32 devices in a mesh: seq: 8 (over z, y), ctx: 4 (over x, core).
Axes of the slice: x: 2, y: 2, z: 4, core: 2. Of those that a mesh axis runs over, the one named last changes fastest.
Arguments:
- hidden_in: bfloat16 [8, 512, 1024], P('seq', 'ctx'), may hold values from -6 to 6
- positions: int32 [8, 512], P('seq', 'ctx'), may hold values from 0 to 499, as said below
- norm1_gain: float32 [1024], replicated, may hold values from 0.5 to 1.5
- w_query: bfloat16 [1024, 2048], P(('seq', 'ctx')), may hold values from -0.1875 to 0.1875
- key_weight_matrix: bfloat16 [1024, 1024], P(('seq', 'ctx')), may hold values from -0.1875 to 0.1875
- value_weight_matrix: bfloat16 [1024, 1024], P(('seq', 'ctx')), may hold values from -0.1875 to 0.1875
- query_gain: float32 [128], replicated, may hold values from 0.8 to 6
- key_gain: float32 [128], replicated, may hold values from 0.8 to 6
- w_out: bfloat16 [1024, 2048], P(('seq', 'ctx')), may hold values from -0.75 to 0.75
- norm2_gain: float32 [1024], replicated, may hold values from 0.5 to 1.5
- w_gate: bfloat16 [1024, 3072], P(('seq', 'ctx')), may hold values from -0.1875 to 0.1875
- w_up: bfloat16 [1024, 3072], P(('seq', 'ctx')), may hold values from -0.1875 to 0.1875
- w_down: bfloat16 [1024, 3072], P(('seq', 'ctx')), may hold values from -0.109375 to 0.109375
- cotangent: bfloat16 [8, 512, 1024], P('seq', 'ctx'), may hold values from -6 to 6
Outputs:
- out_hidden: bfloat16 [8, 512, 1024], P('seq', 'ctx')
- grad_hidden: bfloat16 [8, 512, 1024], P('seq', 'ctx')
- grad_query: float32 [1024, 2048], P(('seq', 'ctx'))
- grad_key: float32 [1024, 1024], P(('seq', 'ctx'))
- grad_value: float32 [1024, 1024], P(('seq', 'ctx'))
- grad_out: float32 [1024, 2048], P(('seq', 'ctx'))
- grad_gate: float32 [1024, 3072], P(('seq', 'ctx'))
- grad_up: float32 [1024, 3072], P(('seq', 'ctx'))
- grad_down: float32 [1024, 3072], P(('seq', 'ctx'))
- grad_norm1: float32 [1024], replicated
- grad_norm2: float32 [1024], replicated
- grad_query_gain: float32 [128], replicated
- grad_key_gain: float32 [128], replicated
The draws below stay inside these ranges and needn't reach their ends.
Inputs may be any that keep to these rules, and one draw needn't show every extreme that they name: In each sequence positions are 0 at the first token and rise by one from token to token, except at the first token of a document, where they return to 0.
All inputs are finite; a program needn't handle non-finite values.
Results may differ from the reference program's by a relative error of at most 0.04.
The reference program's roundings to bfloat16 on the way count: a program that leaves them out, or rounds other values in their place, can miss the bound.
Values may be sent and summed in bfloat16 or wider, within the bound.
No kernel may reach another device: no remote copies, remote signals or barrier semaphores. Data moves between devices by JAX's collectives and lax.ppermute only.
A program may use at most 384 MiB of HBM per device.

```python
import jax
import jax.numpy as jnp
from jax import lax

MODEL_WIDTH = 1024
QUERY_HEADS = 16
KEY_VALUE_HEADS = 8
HEAD_SIZE = 128
FF = 3072
LEN = 512
SEQS = 8
DOC_MIN = 51
DOC_MAX = 500


def draw_positions(key, part):
    doc_count = LEN // DOC_MIN + 1
    lengths = jax.random.randint(key, (SEQS, doc_count), DOC_MIN, DOC_MAX + 1).astype(jnp.int32)
    lengths = lengths.at[0, 0].set(DOC_MAX)
    bounds = jnp.cumsum(lengths, axis=1)
    starts = jnp.concatenate((jnp.zeros((SEQS, 1), jnp.int32), bounds[:, :-1]), 1)
    index = jnp.arange(LEN, dtype=jnp.int32)
    after = starts[:, None, :] <= index[None, :, None]
    begin = jnp.max(jnp.where(after, starts[:, None, :], 0), axis=2)
    return (index[None, :] - begin).astype(jnp.int32)


def draw_query_gain(key, part):
    sub_key = jax.random.fold_in(key, 11)
    return jax.random.uniform(sub_key, (HEAD_SIZE,), jnp.float32, 0.8, 1.6)


def draw_key_gain(key, part):
    sub_key = jax.random.fold_in(key, 12)
    return jax.random.uniform(sub_key, (HEAD_SIZE,), jnp.float32, 0.8, 1.6)


def levels(stream_key, shape, pieces, low, top_value):
    def one(axis_at, blocks):
        draws = jax.random.uniform(jax.random.fold_in(jax.random.fold_in(stream_key, 6), axis_at), (blocks,), jnp.float32, low / len(pieces), top_value / len(pieces))
        return jnp.repeat(jnp.exp(draws), shape[axis_at] // blocks).reshape((-1,) + (1,) * (len(shape) - axis_at - 1))

    loudness = one(*pieces[0])
    for cut in pieces[1:]:
        loudness = loudness * one(*cut)
    return loudness


def normal_values(key, dims, width, reach, shards=(), held_as=jnp.bfloat16):
    values = jax.random.normal(key, dims, jnp.float32) * width
    if len(shards) > 0:
        values = levels(key, dims, shards, -0.22, 0.18) * values
    return jnp.clip(values, min=-reach, max=reach).astype(held_as)


def setup_inputs(seed: int = 0) -> dict:
    keys = jax.random.split(jax.random.key(seed), 15)
    return {
        "hidden_in": normal_values(keys[0], (SEQS, LEN, MODEL_WIDTH), 1.0, 6.0, ((0, 8), (1, 4))),
        "positions": draw_positions(jax.random.fold_in(keys[14], 71), 0),
        "norm1_gain": jnp.clip(1.0 + 0.1 * jax.random.normal(keys[2], (MODEL_WIDTH,), jnp.float32), 0.5, 1.5),
        "w_query": normal_values(keys[3], (MODEL_WIDTH, QUERY_HEADS * HEAD_SIZE), MODEL_WIDTH ** -0.5, 0.1875, ((0, 32),)),
        "key_weight_matrix": normal_values(keys[4], (MODEL_WIDTH, KEY_VALUE_HEADS * HEAD_SIZE), MODEL_WIDTH ** -0.5, 0.1875, ((0, 32),)),
        "value_weight_matrix": normal_values(keys[5], (MODEL_WIDTH, KEY_VALUE_HEADS * HEAD_SIZE), MODEL_WIDTH ** -0.5, 0.1875, ((0, 32),)),
        "query_gain": draw_query_gain(jax.random.fold_in(keys[14], 71), 0),
        "key_gain": draw_key_gain(jax.random.fold_in(keys[14], 71), 0),
        "w_out": normal_values(keys[8], (MODEL_WIDTH, QUERY_HEADS * HEAD_SIZE), (HEAD_SIZE // 2) ** -0.5, 0.75, ((0, 32),)),
        "norm2_gain": jnp.clip(1.0 + 0.1 * jax.random.normal(keys[9], (MODEL_WIDTH,), jnp.float32), 0.5, 1.5),
        "w_gate": normal_values(keys[10], (MODEL_WIDTH, FF), MODEL_WIDTH ** -0.5, 0.1875, ((0, 32),)),
        "w_up": normal_values(keys[11], (MODEL_WIDTH, FF), MODEL_WIDTH ** -0.5, 0.1875, ((0, 32),)),
        "w_down": normal_values(keys[12], (MODEL_WIDTH, FF), FF ** -0.5, 0.109375, ((0, 32),)),
        "cotangent": normal_values(keys[13], (SEQS, LEN, MODEL_WIDTH), 1.0, 6.0, ((0, 8), (1, 4))),
    }


NORM_EPSILON = 1e-06
ROPE_THETA = 1000000.0

def rope_tables(position_ids, head_width):
    half_width = head_width // 2
    inverse = ROPE_THETA ** (-(2.0 / head_width) * jnp.arange(half_width, dtype=jnp.float32))
    angles = position_ids.astype(jnp.float32)[:, None] * inverse[None, :]
    return (jnp.cos(angles), jnp.sin(angles))

def rotate(vectors, cosine, sine):
    half_width = vectors.shape[-1] // 2
    first = vectors[..., :half_width]
    second = vectors[..., half_width:]
    cos_rows = cosine[:, None, :]
    sin_rows = sine[:, None, :]
    return jnp.concatenate((first * cos_rows - second * sin_rows, second * cos_rows + first * sin_rows), -1)

def rotate_back(grads, cosine, sine):
    half_width = grads.shape[-1] // 2
    first = grads[..., :half_width]
    second = grads[..., half_width:]
    cos_rows = cosine[:, None, :]
    sin_rows = sine[:, None, :]
    return jnp.concatenate((first * cos_rows + second * sin_rows, second * cos_rows - first * sin_rows), -1)

def unit_rows(vectors):
    factor = lax.rsqrt(lax.optimization_barrier(jnp.mean(vectors * vectors, -1, keepdims=True)) + NORM_EPSILON)
    return (factor, vectors * factor)

def unit_back(grad_unit, factor, unit):
    return factor * (grad_unit - unit * lax.optimization_barrier(jnp.mean(grad_unit * unit, -1, keepdims=True)))

def sequence_pass(hidden, position_ids, grad_out_b, norm1_gain, w_joint, query_gain, key_gain, w_out, norm2_gain, w_gate, w_up, w_down):
    sequence_length = hidden.shape[0]
    query_columns = QUERY_HEADS * HEAD_SIZE
    key_value_columns = KEY_VALUE_HEADS * HEAD_SIZE
    query_group_count = QUERY_HEADS // KEY_VALUE_HEADS
    inputs = hidden.astype(jnp.float32)
    factor1, unit1 = unit_rows(inputs)
    normed1 = (unit1 * norm1_gain).astype(jnp.bfloat16)
    projected_output = jnp.dot(normed1, w_joint, preferred_element_type=jnp.float32)
    query_raw = projected_output[:, :query_columns].reshape(sequence_length, QUERY_HEADS, HEAD_SIZE)
    unrotated_key = projected_output[:, query_columns:query_columns + key_value_columns].reshape(sequence_length, KEY_VALUE_HEADS, HEAD_SIZE)
    unprojected_value = projected_output[:, query_columns + key_value_columns:].reshape(sequence_length, KEY_VALUE_HEADS, HEAD_SIZE)
    query_factor, query_unit = unit_rows(query_raw)
    key_factor, key_unit = unit_rows(unrotated_key)
    cosine, sine = rope_tables(position_ids, HEAD_SIZE)
    rotated_query = rotate(query_unit * query_gain, cosine, sine).astype(jnp.bfloat16)
    key_rot = rotate(key_unit * key_gain, cosine, sine).astype(jnp.bfloat16)
    values = unprojected_value.astype(jnp.bfloat16)
    query_head_rows = rotated_query.reshape(sequence_length, KEY_VALUE_HEADS, query_group_count, HEAD_SIZE).transpose(1, 2, 0, 3)
    key_heads = key_rot.transpose(1, 0, 2)
    value_heads = values.transpose(1, 0, 2)
    index = jnp.arange(sequence_length, dtype=jnp.int32)
    begin = index - position_ids.astype(jnp.int32)
    allowed = (index[None, :] <= index[:, None]) & (index[None, :] >= begin[:, None])
    score_scale = HEAD_SIZE ** (-0.5)

    def scores_of(query_group, key_group):
        scores = score_scale * jnp.einsum('rtd,sd->rts', query_group.astype(jnp.float32), key_group.astype(jnp.float32))
        return jnp.where(allowed[None], scores, -jnp.inf)

    def attend(operands):
        query_group, key_group, value_group = operands
        scores = scores_of(query_group, key_group)
        highest = lax.optimization_barrier(jnp.max(scores, -1, keepdims=True))
        log_total = highest[..., 0] + jnp.log(lax.optimization_barrier(jnp.sum(jnp.exp(scores - highest), -1)))
        weights = jnp.exp(scores - log_total[..., None]).astype(jnp.bfloat16)
        result = jnp.einsum('rts,sd->rtd', weights.astype(jnp.float32), value_group.astype(jnp.float32))
        return (result, log_total)
    attn_heads, log_total = lax.map(attend, (query_head_rows, key_heads, value_heads))
    attention_row_block = attn_heads.astype(jnp.bfloat16).transpose(2, 0, 1, 3).reshape(sequence_length, query_columns)
    attn_out = jnp.dot(attention_row_block, w_out.T, preferred_element_type=jnp.float32)
    residual = inputs + attn_out
    factor2, unit2 = unit_rows(residual)
    normed2 = (unit2 * norm2_gain).astype(jnp.bfloat16)
    gate = jnp.dot(normed2, w_gate, preferred_element_type=jnp.float32)
    upward = jnp.dot(normed2, w_up, preferred_element_type=jnp.float32)
    sigmoid = jax.nn.sigmoid(gate)
    activation = gate * sigmoid
    hidden_units = (activation * upward).astype(jnp.bfloat16)
    mlp_out = jnp.dot(hidden_units, w_down.T, preferred_element_type=jnp.float32)
    out_hidden = (residual + mlp_out).astype(jnp.bfloat16)
    grad_hidden = jnp.dot(grad_out_b, w_down, preferred_element_type=jnp.float32)
    grad_gate = (grad_hidden * upward * sigmoid * (1.0 + gate * (1.0 - sigmoid))).astype(jnp.bfloat16)
    grad_up = (grad_hidden * activation).astype(jnp.bfloat16)
    grad_normed2 = jnp.dot(grad_gate, w_gate.T, preferred_element_type=jnp.float32) + jnp.dot(grad_up, w_up.T, preferred_element_type=jnp.float32)
    gain2_term = lax.optimization_barrier(jnp.sum(grad_normed2 * unit2, 0))
    grad_residual = grad_out_b.astype(jnp.float32) + unit_back(grad_normed2 * norm2_gain, factor2, unit2)
    grad_residual_b = grad_residual.astype(jnp.bfloat16)
    attention_gradient_backward = jnp.dot(grad_residual_b, w_out, preferred_element_type=jnp.float32).astype(jnp.bfloat16)
    head_gradient = attention_gradient_backward.reshape(sequence_length, KEY_VALUE_HEADS, query_group_count, HEAD_SIZE).transpose(1, 2, 0, 3)
    attention_heads_backward = attention_row_block.reshape(sequence_length, KEY_VALUE_HEADS, query_group_count, HEAD_SIZE).transpose(1, 2, 0, 3)
    delta_rows = lax.optimization_barrier(jnp.sum(head_gradient.astype(jnp.float32) * attention_heads_backward.astype(jnp.float32), -1))

    def attend_back(operands):
        query_group, key_group, value_group, grad_group, lse_group, delta_group = operands
        scores = scores_of(query_group, key_group)
        probs = jnp.exp(scores - lse_group[..., None])
        probability_backward = probs.astype(jnp.bfloat16)
        grad_probs = jnp.einsum('rtd,sd->rts', grad_group.astype(jnp.float32), value_group.astype(jnp.float32))
        score_gradient = (probs * (grad_probs - delta_group[..., None])).astype(jnp.bfloat16)
        grad_q = score_scale * jnp.einsum('rts,sd->rtd', score_gradient.astype(jnp.float32), key_group.astype(jnp.float32))
        grad_k = score_scale * jnp.einsum('rts,rtd->sd', score_gradient.astype(jnp.float32), query_group.astype(jnp.float32))
        grad_v = jnp.einsum('rts,rtd->sd', probability_backward.astype(jnp.float32), grad_group.astype(jnp.float32))
        return (grad_q, grad_k, grad_v)
    grad_q_heads, grad_k_heads, grad_v_heads = lax.map(attend_back, (query_head_rows, key_heads, value_heads, head_gradient, log_total, delta_rows))
    grad_query = rotate_back(grad_q_heads.transpose(2, 0, 1, 3).reshape(sequence_length, QUERY_HEADS, HEAD_SIZE), cosine, sine)
    grad_key = rotate_back(grad_k_heads.transpose(1, 0, 2), cosine, sine)
    grad_value = grad_v_heads.transpose(1, 0, 2)
    qgain_term = lax.optimization_barrier(jnp.sum(grad_query * query_unit, (0, 1)))
    kgain_term = lax.optimization_barrier(jnp.sum(grad_key * key_unit, (0, 1)))
    grad_query_raw = unit_back(grad_query * query_gain, query_factor, query_unit)
    grad_key_raw = unit_back(grad_key * key_gain, key_factor, key_unit)
    grad_joint = jnp.concatenate((grad_query_raw.reshape(sequence_length, query_columns), grad_key_raw.reshape(sequence_length, key_value_columns), grad_value.reshape(sequence_length, key_value_columns)), 1).astype(jnp.bfloat16)
    grad_normed1 = jnp.dot(grad_joint, w_joint.T, preferred_element_type=jnp.float32)
    gain1_term = lax.optimization_barrier(jnp.sum(grad_normed1 * unit1, 0))
    grad_inputs = (grad_residual + unit_back(grad_normed1 * norm1_gain, factor1, unit1)).astype(jnp.bfloat16)
    terms = (jnp.dot(normed1.T, grad_joint, preferred_element_type=jnp.float32), jnp.dot(grad_residual_b.T, attention_row_block, preferred_element_type=jnp.float32), jnp.dot(normed2.T, grad_gate, preferred_element_type=jnp.float32), jnp.dot(normed2.T, grad_up, preferred_element_type=jnp.float32), jnp.dot(grad_out_b.T, hidden_units, preferred_element_type=jnp.float32), gain1_term, gain2_term, qgain_term, kgain_term)
    return (out_hidden, grad_inputs, terms)

def reference(hidden_in, positions, norm1_gain, w_query, key_weight_matrix, value_weight_matrix, query_gain, key_gain, w_out, norm2_gain, w_gate, w_up, w_down, cotangent):
    query_columns = QUERY_HEADS * HEAD_SIZE
    key_value_columns = KEY_VALUE_HEADS * HEAD_SIZE
    w_joint = jnp.concatenate((w_query, key_weight_matrix, value_weight_matrix), 1)

    def step_one(totals, items):
        hidden, position_ids, grad_out_b = items
        out_hidden, grad_inputs, terms = sequence_pass(hidden, position_ids, grad_out_b, norm1_gain, w_joint, query_gain, key_gain, w_out, norm2_gain, w_gate, w_up, w_down)
        totals = tuple((total + term for total, term in zip(totals, terms)))
        return (totals, (out_hidden, grad_inputs))
    start_totals = (jnp.zeros((MODEL_WIDTH, query_columns + 2 * key_value_columns), jnp.float32), jnp.zeros((MODEL_WIDTH, query_columns), jnp.float32), jnp.zeros((MODEL_WIDTH, FF), jnp.float32), jnp.zeros((MODEL_WIDTH, FF), jnp.float32), jnp.zeros((MODEL_WIDTH, FF), jnp.float32), jnp.zeros((MODEL_WIDTH,), jnp.float32), jnp.zeros((MODEL_WIDTH,), jnp.float32), jnp.zeros((HEAD_SIZE,), jnp.float32), jnp.zeros((HEAD_SIZE,), jnp.float32))
    totals, (out_hidden, grad_hidden) = lax.scan(step_one, start_totals, (hidden_in, positions, cotangent))
    joint_grad = totals[0]
    return (out_hidden, grad_hidden, joint_grad[:, :query_columns], joint_grad[:, query_columns:query_columns + key_value_columns], joint_grad[:, query_columns + key_value_columns:], totals[1], totals[2], totals[3], totals[4], totals[5], totals[6], totals[7], totals[8])
```

```python
import functools

import jax
import jax.numpy as jnp
from jax import lax
from jax.experimental import pallas as pl
from jax.experimental.pallas import tpu as pltpu
from jax.sharding import PartitionSpec as P

NORM_EPSILON = 1e-06
ROPE_THETA = 1000000.0


def rope_tables(position_ids, head_width):
    half_width = head_width // 2
    inverse = ROPE_THETA ** (-(2.0 / head_width) * jnp.arange(half_width, dtype=jnp.float32))
    angles = position_ids.astype(jnp.float32)[:, None] * inverse[None, :]
    return (jnp.cos(angles), jnp.sin(angles))


def rotate(vectors, cosine, sine):
    half_width = vectors.shape[-1] // 2
    first = vectors[..., :half_width]
    second = vectors[..., half_width:]
    cos_rows = cosine[:, None, :]
    sin_rows = sine[:, None, :]
    return jnp.concatenate(
        (first * cos_rows - second * sin_rows, second * cos_rows + first * sin_rows), -1
    )


def rotate_back(grads, cosine, sine):
    half_width = grads.shape[-1] // 2
    first = grads[..., :half_width]
    second = grads[..., half_width:]
    cos_rows = cosine[:, None, :]
    sin_rows = sine[:, None, :]
    return jnp.concatenate(
        (first * cos_rows + second * sin_rows, second * cos_rows - first * sin_rows), -1
    )


def unit_rows(vectors):
    factor = lax.rsqrt(jnp.mean(vectors * vectors, -1, keepdims=True) + NORM_EPSILON)
    return (factor, vectors * factor)


def unit_back(grad_unit, factor, unit):
    return factor * (grad_unit - unit * jnp.mean(grad_unit * unit, -1, keepdims=True))


def outer_rows(left, right):
    return jnp.einsum("tj,tc->jc", left, right, preferred_element_type=jnp.float32)


def gathered_layer(
    hidden_in,
    positions,
    norm1_gain,
    w_query,
    key_weight_matrix,
    value_weight_matrix,
    query_gain,
    key_gain,
    w_out,
    norm2_gain,
    w_gate,
    w_up,
    w_down,
    cotangent,
):
    row_count = hidden_in.shape[1]
    head_width = query_gain.shape[0]
    query_columns = w_query.shape[1]
    key_value_columns = key_weight_matrix.shape[1]
    kv_heads = key_value_columns // head_width
    query_group_count = query_columns // key_value_columns
    attn_width = query_columns + 2 * key_value_columns + query_columns
    inputs = hidden_in[0].astype(jnp.float32)
    position_ids = positions[0]
    factor1, unit1 = unit_rows(inputs)
    normed1 = (unit1 * norm1_gain).astype(jnp.bfloat16)
    w_joint = jnp.concatenate((w_query, key_weight_matrix, value_weight_matrix), 1)
    joint_full, out_full = (
        lax.all_gather(w_joint, ("seq", "ctx"), axis=0, tiled=True),
        lax.all_gather(w_out, ("seq", "ctx"), axis=0, tiled=True),
    )
    projected_output = jnp.dot(normed1, joint_full, preferred_element_type=jnp.float32)
    query_raw = projected_output[:, :query_columns].reshape(
        row_count, query_columns // head_width, head_width
    )
    unrotated_key = projected_output[:, query_columns : query_columns + key_value_columns].reshape(
        row_count, kv_heads, head_width
    )
    unprojected_value = projected_output[:, query_columns + key_value_columns :].reshape(
        row_count, kv_heads, head_width
    )
    query_factor, query_unit = unit_rows(query_raw)
    key_factor, key_unit = unit_rows(unrotated_key)
    cosine, sine = rope_tables(position_ids, head_width)
    rotated_query = rotate(query_unit * query_gain, cosine, sine).astype(jnp.bfloat16)
    key_rot = rotate(key_unit * key_gain, cosine, sine).astype(jnp.bfloat16)
    query_head_rows = rotated_query.reshape(
        row_count, kv_heads, query_group_count, head_width
    ).transpose(1, 2, 0, 3)
    own_pair = jnp.stack((key_rot, unprojected_value.astype(jnp.bfloat16)))
    cycle_size = lax.axis_size("ctx")
    my_block = lax.axis_index("ctx")
    offsets = jnp.arange(row_count, dtype=jnp.int32)
    query_index = my_block * row_count + offsets
    doc_begin = query_index - position_ids
    score_scale = head_width ** (-0.5)

    def visible(count):
        key_index = jnp.arange(count, dtype=jnp.int32)
        return (key_index[None, :] <= query_index[:, None]) & (
            key_index[None, :] >= doc_begin[:, None]
        )

    def block_scores(key_value_couple, key_mask):
        scores = score_scale * jnp.einsum(
            "ekla,xea->eklx",
            query_head_rows,
            key_value_couple[0],
            preferred_element_type=jnp.float32,
        )
        return jnp.where(key_mask[None, None], scores, -jnp.inf)

    state = (
        jnp.full((kv_heads, query_group_count, row_count), -jnp.inf, jnp.float32),
        jnp.zeros((kv_heads, query_group_count, row_count), jnp.float32),
        jnp.zeros((kv_heads, query_group_count, row_count, head_width), jnp.float32),
    )
    key_value_couple = lax.all_gather(own_pair, "ctx", axis=1, tiled=True)
    key_mask = visible(key_value_couple.shape[1])

    def attend(current):
        highest, totals, accum = current
        scores = block_scores(key_value_couple, key_mask)
        new_high = jnp.max(scores, -1)
        decay = jnp.exp(highest - new_high)
        weights = jnp.exp(scores - new_high[..., None])
        totals = totals * decay + jnp.sum(weights, -1)
        accum = accum * decay[..., None] + jnp.einsum(
            "emaj,jep->emap",
            weights.astype(jnp.bfloat16),
            key_value_couple[1],
            preferred_element_type=jnp.float32,
        )
        return (new_high, totals, accum)

    highest, totals, accum = lax.cond(jnp.any(key_mask), attend, lambda current: current, state)
    log_total = highest + jnp.log(totals)
    attn_heads = (accum / totals[..., None]).astype(jnp.bfloat16)
    attention_row_block = attn_heads.transpose(2, 0, 1, 3).reshape(row_count, query_columns)
    attn_out = jnp.einsum(
        "tc,jc->tj", attention_row_block, out_full, preferred_element_type=jnp.float32
    )
    residual = inputs + attn_out
    factor2, unit2 = unit_rows(residual)
    normed2 = (unit2 * norm2_gain).astype(jnp.bfloat16)
    gate_full, up_full, down_full = (
        lax.all_gather(w_gate, ("seq", "ctx"), axis=0, tiled=True),
        lax.all_gather(w_up, ("seq", "ctx"), axis=0, tiled=True),
        lax.all_gather(w_down, ("seq", "ctx"), axis=0, tiled=True),
    )
    gate = jnp.dot(normed2, gate_full, preferred_element_type=jnp.float32)
    upward = jnp.dot(normed2, up_full, preferred_element_type=jnp.float32)
    sigmoid = jax.nn.sigmoid(gate)
    activation = gate * sigmoid
    hidden_units = (activation * upward).astype(jnp.bfloat16)
    mlp_out = jnp.einsum("tf,jf->tj", hidden_units, down_full, preferred_element_type=jnp.float32)
    out_hidden = (residual + mlp_out).astype(jnp.bfloat16)
    grad_out_b = cotangent[0]
    grad_hidden = jnp.dot(grad_out_b, down_full, preferred_element_type=jnp.float32)
    grad_gate = (grad_hidden * upward * sigmoid * (1.0 + gate * (1.0 - sigmoid))).astype(
        jnp.bfloat16
    )
    grad_up = (grad_hidden * activation).astype(jnp.bfloat16)
    grad_normed2 = jnp.einsum(
        "tf,jf->tj", grad_gate, gate_full, preferred_element_type=jnp.float32
    ) + jnp.einsum("tf,jf->tj", grad_up, up_full, preferred_element_type=jnp.float32)
    gain2_local = jnp.sum(grad_normed2 * unit2, 0)
    grad_residual = grad_out_b.astype(jnp.float32) + unit_back(
        grad_normed2 * norm2_gain, factor2, unit2
    )
    grad_residual_b = grad_residual.astype(jnp.bfloat16)
    grad_attn = jnp.dot(grad_residual_b, out_full, preferred_element_type=jnp.float32)
    attention_gradient_backward = grad_attn.astype(jnp.bfloat16)
    head_gradient = attention_gradient_backward.reshape(
        row_count, kv_heads, query_group_count, head_width
    ).transpose(1, 2, 0, 3)
    delta_rows = jnp.sum(head_gradient.astype(jnp.float32) * attn_heads.astype(jnp.float32), -1)
    grads_full = jnp.zeros((2, row_count * cycle_size, kv_heads, head_width), jnp.float32)
    grad_q_acc = jnp.zeros((kv_heads, query_group_count, row_count, head_width), jnp.float32)
    current = (grads_full, grad_q_acc)
    backward_key_value_couple = lax.all_gather(own_pair, "ctx", axis=1, tiled=True)
    piece_rows = backward_key_value_couple.shape[1]
    backward_key_mask = visible(piece_rows)

    def attend_back(inner):
        scores = block_scores(backward_key_value_couple, backward_key_mask)
        probs = jnp.exp(scores - log_total[..., None])
        probability_backward = probs.astype(jnp.bfloat16)
        grad_probs = jnp.einsum(
            "ekla,xea->eklx",
            head_gradient,
            backward_key_value_couple[1],
            preferred_element_type=jnp.float32,
        )
        score_gradient = (probs * (grad_probs - delta_rows[..., None])).astype(jnp.bfloat16)
        grad_q_acc = score_scale * jnp.einsum(
            "emaj,jep->emap",
            score_gradient,
            backward_key_value_couple[0],
            preferred_element_type=jnp.float32,
        )
        grad_keys = score_scale * jnp.einsum(
            "kejx,kejy->xky", score_gradient, query_head_rows, preferred_element_type=jnp.float32
        )
        grad_values = jnp.einsum(
            "kejx,kejy->xky",
            probability_backward,
            head_gradient,
            preferred_element_type=jnp.float32,
        )
        grads_full = jnp.stack((grad_keys, grad_values))
        return (grads_full, grad_q_acc)

    grads_full, grad_q_acc = lax.cond(
        jnp.any(backward_key_mask), attend_back, lambda inner: inner, current
    )
    grads_kv = lax.psum_scatter(
        grads_full.astype(jnp.bfloat16), "ctx", scatter_dimension=1, tiled=True
    ).astype(jnp.float32)
    grad_query = rotate_back(
        grad_q_acc.transpose(2, 0, 1, 3).reshape(
            row_count, query_columns // head_width, head_width
        ),
        cosine,
        sine,
    )
    grad_key = rotate_back(grads_kv[0], cosine, sine)
    qgain_local = jnp.sum(grad_query * query_unit, (0, 1))
    kgain_local = jnp.sum(grad_key * key_unit, (0, 1))
    grad_query_raw = unit_back(grad_query * query_gain, query_factor, query_unit)
    grad_key_raw = unit_back(grad_key * key_gain, key_factor, key_unit)
    grad_joint = jnp.concatenate(
        (
            grad_query_raw.reshape(row_count, query_columns),
            grad_key_raw.reshape(row_count, key_value_columns),
            grads_kv[1].reshape(row_count, key_value_columns),
        ),
        1,
    ).astype(jnp.bfloat16)
    grad_normed1 = jnp.einsum(
        "tc,jc->tj", grad_joint, joint_full, preferred_element_type=jnp.float32
    )
    gain1_local = jnp.sum(grad_normed1 * unit1, 0)
    grad_inputs = (grad_residual + unit_back(grad_normed1 * norm1_gain, factor1, unit1)).astype(
        jnp.bfloat16
    )
    joined = lax.psum_scatter(
        jnp.concatenate(
            (
                jnp.concatenate(
                    (
                        outer_rows(normed1, grad_joint),
                        outer_rows(grad_residual_b, attention_row_block),
                    ),
                    1,
                ),
                jnp.concatenate(
                    (
                        outer_rows(normed2, grad_gate),
                        outer_rows(normed2, grad_up),
                        outer_rows(grad_out_b, hidden_units),
                    ),
                    1,
                ),
            ),
            1,
        ),
        ("seq", "ctx"),
        scatter_dimension=0,
        tiled=True,
    )
    attn_grads = joined[:, :attn_width]
    mlp_grads = joined[:, attn_width:]
    gain_totals = lax.psum((gain1_local, gain2_local, qgain_local, kgain_local), ("seq", "ctx"))
    hidden_width = w_gate.shape[1]
    return (
        out_hidden[None],
        grad_inputs[None],
        attn_grads[:, :query_columns],
        attn_grads[:, query_columns : query_columns + key_value_columns],
        attn_grads[:, query_columns + key_value_columns : query_columns + 2 * key_value_columns],
        attn_grads[:, query_columns + 2 * key_value_columns :],
        mlp_grads[:, :hidden_width],
        mlp_grads[:, hidden_width : 2 * hidden_width],
        mlp_grads[:, 2 * hidden_width :],
        gain_totals[0],
        gain_totals[1],
        gain_totals[2],
        gain_totals[3],
    )


def turn(rows, cosine, sine):
    return rows * cosine + pltpu.roll(rows, rows.shape[-1] // 2, 1) * sine


def head_rows(raw, gain, cosine, sine):
    factor, unit = unit_rows(raw)
    return factor, unit, turn(unit * gain, cosine, sine).astype(jnp.bfloat16)


def dot_of(left, right, left_dim, right_dim):
    return lax.dot_general(
        left, right, (((left_dim,), (right_dim,)), ((), ())), preferred_element_type=jnp.float32
    )


def probabilities(key_rot, query_rot, mask):
    scores = dot_of(key_rot, query_rot, 1, 1) * key_rot.shape[-1] ** (-0.5) + mask
    weights = jnp.exp(scores - jnp.max(scores, 0, keepdims=True))
    return weights / jnp.sum(weights, 0, keepdims=True)


def attend_kernel(group, width, q_ref, k_ref, v_ref, mask_ref, cos_ref, sin_ref, qg_ref, kg_ref, o_ref):
    cosine, sine = cos_ref[...], sin_ref[...]
    key_rot = head_rows(k_ref[...], kg_ref[...], cosine, sine)[2]
    value = v_ref[...].astype(jnp.bfloat16)
    for r in range(group):
        cols = slice(r * width, (r + 1) * width)
        query_rot = head_rows(q_ref[:, cols], qg_ref[...], cosine, sine)[2]
        probs = probabilities(key_rot, query_rot, mask_ref[...]).astype(jnp.bfloat16)
        o_ref[:, cols] = dot_of(value, probs, 0, 0).T.astype(jnp.bfloat16)


def attend_back_kernel(
    group, width, q_ref, k_ref, v_ref, attn_ref, grad_ref, mask_ref, cos_ref, sin_ref,
    qg_ref, kg_ref, dq_ref, dk_ref, dv_ref, gain_ref,
):
    cosine, sine = cos_ref[...], sin_ref[...]
    scale = width ** (-0.5)
    key_factor, key_unit, key_rot = head_rows(k_ref[...], kg_ref[...], cosine, sine)
    value = v_ref[...].astype(jnp.bfloat16)

    @pl.when(pl.program_id(0) == 0)
    def _():
        gain_ref[...] = jnp.zeros_like(gain_ref)

    grad_key = jnp.zeros(key_rot.shape, jnp.float32)
    grad_value = jnp.zeros(key_rot.shape, jnp.float32)
    for r in range(group):
        cols = slice(r * width, (r + 1) * width)
        query_factor, query_unit, query_rot = head_rows(q_ref[:, cols], qg_ref[...], cosine, sine)
        probs = probabilities(key_rot, query_rot, mask_ref[...])
        grad = grad_ref[:, cols]
        product = grad.astype(jnp.float32) * attn_ref[:, cols].astype(jnp.float32)
        delta = jnp.sum(product.T, 0, keepdims=True)
        grad_scores = (probs * (dot_of(value, grad, 1, 1) - delta)).astype(jnp.bfloat16)
        grad_value += dot_of(probs.astype(jnp.bfloat16), grad, 1, 0)
        grad_key += dot_of(grad_scores, query_rot, 1, 0)
        grad_query = turn(scale * dot_of(key_rot, grad_scores, 0, 0).T, cosine, -sine)
        gain_ref[0:1, :] += jnp.sum(grad_query * query_unit, 0, keepdims=True)
        dq_ref[:, cols] = unit_back(grad_query * qg_ref[...], query_factor, query_unit).astype(
            jnp.bfloat16
        )
    grad_key = turn(scale * grad_key, cosine, -sine)
    gain_ref[1:2, :] += jnp.sum(grad_key * key_unit, 0, keepdims=True)
    dk_ref[...] = unit_back(grad_key * kg_ref[...], key_factor, key_unit).astype(jnp.bfloat16)
    dv_ref[...] = grad_value.astype(jnp.bfloat16)


def attend_specs(tokens, width, heads, kv_heads):
    group = heads // kv_heads
    query = pl.BlockSpec((tokens, group * width), lambda h: (0, h))
    own = pl.BlockSpec((tokens, width), lambda h: (0, h))
    key = pl.BlockSpec((tokens, width), lambda h: (0, heads + h))
    value = pl.BlockSpec((tokens, width), lambda h: (0, heads + kv_heads + h))
    square = pl.BlockSpec((tokens, tokens), lambda h: (0, 0))
    table = pl.BlockSpec((tokens, width), lambda h: (0, 0))
    gain = pl.BlockSpec((1, width), lambda h: (0, 0))
    return query, own, key, value, square, table, gain


def attend(projected, mask, cosine, sine, gains, heads, kv_heads):
    tokens, width = cosine.shape
    query, own, key, value, square, table, gain = attend_specs(tokens, width, heads, kv_heads)
    return pl.pallas_call(
        functools.partial(attend_kernel, heads // kv_heads, width),
        grid=(kv_heads,),
        in_specs=[query, key, value, square, table, table, gain, gain],
        out_specs=query,
        out_shape=jax.ShapeDtypeStruct((tokens, heads * width), jnp.bfloat16),
        name="attend",
    )(projected, projected, projected, mask, cosine, sine, *gains)


def attend_back(projected, attn, grad_attn, mask, cosine, sine, gains, heads, kv_heads):
    tokens, width = cosine.shape
    query, own, key, value, square, table, gain = attend_specs(tokens, width, heads, kv_heads)
    kv_shape = jax.ShapeDtypeStruct((tokens, kv_heads * width), jnp.bfloat16)
    grad_q, grad_k, grad_v, gain_sums = pl.pallas_call(
        functools.partial(attend_back_kernel, heads // kv_heads, width),
        grid=(kv_heads,),
        in_specs=[query, key, value, query, query, square, table, table, gain, gain],
        out_specs=[query, own, own, pl.BlockSpec((8, width), lambda h: (0, 0))],
        out_shape=[
            jax.ShapeDtypeStruct((tokens, heads * width), jnp.bfloat16),
            kv_shape,
            kv_shape,
            jax.ShapeDtypeStruct((8, width), jnp.float32),
        ],
        name="attend_back",
    )(projected, projected, projected, attn, grad_attn, mask, cosine, sine, *gains)
    return jnp.concatenate((grad_q, grad_k, grad_v), 1), gain_sums


def can_slice(mesh):
    seq_size = mesh.shape["seq"]
    ctx_size = mesh.shape["ctx"]
    return seq_size == 8 and ctx_size == 4


def swap_ctx(array, bit, seq_size, ctx_size):
    pairs = [
        (s * ctx_size + c, s * ctx_size + (c ^ bit))
        for s in range(seq_size)
        for c in range(ctx_size)
    ]
    return lax.ppermute(array, ("seq", "ctx"), pairs)


def sliced_layer(
    hidden_in,
    positions,
    norm1_gain,
    w_query,
    key_weight_matrix,
    value_weight_matrix,
    query_gain,
    key_gain,
    w_out,
    norm2_gain,
    w_gate,
    w_up,
    w_down,
    cotangent,
):
    seq_size = lax.axis_size("seq")
    ctx_size = lax.axis_size("ctx")
    my_seq = lax.axis_index("seq")
    my_ctx = lax.axis_index("ctx")
    row_count = hidden_in.shape[1]
    width = hidden_in.shape[2]
    head_width = query_gain.shape[0]
    heads = w_query.shape[1] // head_width // ctx_size
    kv_heads = key_weight_matrix.shape[1] // head_width // ctx_size
    group = heads // kv_heads
    hidden_cols = w_gate.shape[1] // ctx_size
    bits = [1 << b for b in reversed(range(ctx_size.bit_length() - 1))]
    block = width // seq_size
    half = seq_size // 2

    def spot_of(s):
        return jnp.where(s % 2 == 0, s // 2, seq_size - 1 - s // 2)

    ring = list(range(0, seq_size, 2)) + list(range(seq_size - 1, 0, -2))
    spot = spot_of(my_seq)
    offsets = [0]
    for k in range(1, half):
        offsets += [-k, k]
    offsets.append(half)
    place = {o % seq_size: k for k, o in enumerate(offsets)}
    order = []
    for o in offsets:
        r = (spot + (o + seq_size)) % seq_size
        order.append(jnp.where(r < half, 2 * r, 2 * (seq_size - 1 - r) + 1))
    unorder = []
    for s in range(seq_size):
        r = (ring.index(s) + seq_size - spot) % seq_size
        near = jnp.where(r < half, 2 * r, 2 * (seq_size - r) - 1)
        unorder.append(jnp.where(r == half, seq_size - 1, near))

    def pick_blocks(array, which):
        return jnp.concatenate(
            [
                lax.dynamic_slice_in_dim(array, which[k] * block, block, array.ndim - 1)
                for k in range(seq_size)
            ],
            array.ndim - 1,
        )

    def shift(array, by):
        pairs = [
            (
                ring[r] * ctx_size + c,
                ring[(r + by) % seq_size] * ctx_size + c,
            )
            for r in range(seq_size)
            for c in range(ctx_size)
        ]
        return lax.ppermute(array, ("seq", "ctx"), pairs)

    def swap(array, bit):
        return swap_ctx(array, bit, seq_size, ctx_size)

    def exchange(pieces):
        for bit in bits:
            mine = (my_ctx & bit) != 0
            low = [d for d in range(ctx_size) if not d & bit]
            send = jnp.stack([jnp.where(mine, pieces[d], pieces[d | bit]) for d in low])
            keep = [jnp.where(mine, pieces[d | bit], pieces[d]) for d in low]
            got = swap(send, bit)
            pieces = list(pieces)
            for k, d in enumerate(low):
                pieces[d] = jnp.where(mine, got[k], keep[k])
                pieces[d | bit] = jnp.where(mine, keep[k], got[k])
        return pieces

    def join_tokens(array):
        for bit in bits:
            array = jnp.concatenate((array, swap(array, bit)), 0)
        return array

    def sum_tokens(array):
        for bit in reversed(bits):
            rows = array.shape[0] // 2
            got = swap(array[rows:].astype(jnp.bfloat16), bit)
            array = array[:rows] + got.astype(jnp.float32)
        return array

    def gather_rows(own):
        blocks = [own]
        ahead = own
        back = own
        for k in range(1, half):
            ahead = shift(ahead, 1)
            back = shift(back, -1)
            blocks += [ahead, back]
        middle = block // 2
        blocks.append(
            jnp.concatenate((shift(ahead[:middle], 1), shift(back[middle:], -1)), 0)
        )
        return blocks

    def scatter_rows(pairs):
        def rows_of(offset):
            k = place[offset % seq_size]
            return jnp.concatenate(
                [dot(x[:, k * block : (k + 1) * block], g, first) for x, g in pairs], 1
            )

        middle = block // 2
        far = rows_of(half).astype(jnp.bfloat16)
        total = rows_of(0)
        ahead = shift(far[:middle], 1).astype(jnp.float32)
        back = shift(far[middle:], -1).astype(jnp.float32)
        for k in range(half - 1, 0, -1):
            to_ahead = rows_of(k)
            to_back = rows_of(-k)
            if k == half - 1:
                to_ahead = jnp.concatenate((to_ahead[:middle] + ahead, to_ahead[middle:]), 0)
                to_back = jnp.concatenate((to_back[:middle], to_back[middle:] + back), 0)
            else:
                to_ahead = to_ahead + ahead
                to_back = to_back + back
            ahead = shift(to_ahead.astype(jnp.bfloat16), 1).astype(jnp.float32)
            back = shift(to_back.astype(jnp.bfloat16), -1).astype(jnp.float32)
        return total + ahead + back

    def column_pieces(matrices):
        pieces = []
        for d in range(ctx_size):
            parts = []
            for m in matrices:
                n = m.shape[1] // ctx_size
                parts.append(m[:, d * n : (d + 1) * n])
            pieces.append(parts[0] if len(parts) == 1 else jnp.concatenate(parts, 1))
        return pieces

    def own_rows(matrices):
        return jnp.concatenate(exchange(column_pieces(matrices)), 0)

    def after(array, *others):
        return lax.optimization_barrier((array, *others))[0]

    def sum_all(array):
        for bit in bits:
            array = array + swap(array, bit)
        bit = 1
        while bit < seq_size:
            pairs = [
                (s * ctx_size + c, (s ^ bit) * ctx_size + c)
                for s in range(seq_size)
                for c in range(ctx_size)
            ]
            array = array + lax.ppermute(array, ("seq", "ctx"), pairs)
            bit *= 2
        return array

    def collect(pairs, sizes):
        rows = scatter_rows(pairs).astype(jnp.bfloat16)
        small = rows.shape[0] // ctx_size
        pieces = exchange([rows[d * small : (d + 1) * small] for d in range(ctx_size)])
        results = []
        start = 0
        for n in sizes:
            results.append(
                jnp.concatenate([p[:, start : start + n] for p in pieces], 1).astype(jnp.float32)
            )
            start += n
        return results

    def dot(left, right, dims):
        return lax.dot_general(left, right, (dims, ((), ())), preferred_element_type=jnp.float32)

    plain = ((1,), (0,))
    last = ((1,), (1,))
    first = ((0,), (0,))

    gain1 = pick_blocks(norm1_gain, order)
    gain2 = pick_blocks(norm2_gain, order)
    inputs = pick_blocks(hidden_in[0], order).astype(jnp.float32)
    cot_own = pick_blocks(cotangent[0], order)
    factor1, unit1 = unit_rows(inputs)
    digits = jnp.where(
        jnp.arange(head_width)[None, :] < head_width // 2,
        positions[0][:, None] // 128,
        positions[0][:, None] % 128,
    ).astype(jnp.bfloat16)
    attn_own = own_rows([w_query, key_weight_matrix, value_weight_matrix, w_out])
    mlp_own = own_rows([after(w_gate, attn_own), w_up, w_down])
    joined = join_tokens(
        jnp.concatenate(((unit1 * gain1).astype(jnp.bfloat16), cot_own, digits), 1)
    )
    normed1 = joined[:, :width]
    cot = joined[:, width : 2 * width]
    digits = joined[:, 2 * width :].astype(jnp.float32)
    position_ids = (digits[:, 0] * 128.0 + digits[:, head_width // 2]).astype(jnp.int32)

    query_cols = heads * head_width
    kv_cols = kv_heads * head_width
    attn_full = jnp.concatenate(gather_rows(attn_own), 0)
    mlp_full = jnp.concatenate(gather_rows(mlp_own), 0)
    joint = attn_full[:, : query_cols + 2 * kv_cols]
    out_cols = attn_full[:, query_cols + 2 * kv_cols :]
    gate_up = mlp_full[:, : 2 * hidden_cols]
    down = mlp_full[:, 2 * hidden_cols :]

    tokens = row_count * ctx_size
    projected = dot(normed1, joint, plain)
    owners = [0]
    for bit in bits:
        owners = owners + [o ^ bit for o in owners]
    index = jnp.concatenate(
        [(my_ctx ^ o) * row_count + jnp.arange(row_count, dtype=jnp.int32) for o in owners]
    )
    begin = index - position_ids
    allowed = (index[:, None] <= index[None, :]) & (index[:, None] >= begin[None, :])
    mask = jnp.where(allowed, 0.0, -jnp.inf)
    cosine, sine = rope_tables(position_ids, head_width)
    cosine = jnp.concatenate((cosine, cosine), 1)
    sine = jnp.concatenate((-sine, sine), 1)
    gains = (query_gain[None, :], key_gain[None, :])
    attn = attend(projected, mask, cosine, sine, gains, heads, kv_heads)

    residual = inputs + sum_tokens(dot(attn, out_cols, last))
    factor2, unit2 = unit_rows(residual)
    normed2 = join_tokens((unit2 * gain2).astype(jnp.bfloat16))
    gate_up_out = dot(normed2, gate_up, plain)
    gate = gate_up_out[:, :hidden_cols]
    upward = gate_up_out[:, hidden_cols:]
    sigmoid = jax.nn.sigmoid(gate)
    activation = gate * sigmoid
    hidden_units = (activation * upward).astype(jnp.bfloat16)
    grad_hid = dot(cot, down, plain)
    grad_gate = grad_hid * upward * sigmoid * (1.0 + gate * (1.0 - sigmoid))
    grad_up = grad_hid * activation
    grad_gate_up = jnp.concatenate((grad_gate, grad_up), 1).astype(jnp.bfloat16)
    grad_down_w, grad_gate_w, grad_up_w = collect(
        [(cot, hidden_units), (normed2, grad_gate_up)], [hidden_cols] * 3
    )
    out_hidden = (residual + sum_tokens(dot(hidden_units, down, last))).astype(jnp.bfloat16)

    grad_normed2 = sum_tokens(dot(grad_gate_up, gate_up, last))
    gain2_local = jnp.sum(grad_normed2 * unit2, 0)
    grad_residual = cot_own.astype(jnp.float32) + unit_back(grad_normed2 * gain2, factor2, unit2)
    grad_residual_b = join_tokens(grad_residual.astype(jnp.bfloat16))
    grad_attn = dot(grad_residual_b, out_cols, plain).astype(jnp.bfloat16)

    grad_joint, gain_local = attend_back(
        projected, attn, grad_attn, mask, cosine, sine, gains, heads, kv_heads
    )
    grad_out_w, grad_query_w, grad_key_w, grad_value_w = collect(
        [(grad_residual_b, attn), (normed1, grad_joint)],
        [query_cols, query_cols, kv_cols, kv_cols],
    )
    grad_normed1 = sum_tokens(dot(grad_joint, joint, last))
    gain1_local = jnp.sum(grad_normed1 * unit1, 0)
    grad_inputs = (grad_residual + unit_back(grad_normed1 * gain1, factor1, unit1)).astype(
        jnp.bfloat16
    )
    gain_sizes = [width, width, head_width, head_width]
    gain_rows = sum_all(
        jnp.concatenate(
            (
                pick_blocks(gain1_local, unorder),
                pick_blocks(gain2_local, unorder),
                gain_local[0],
                gain_local[1],
            )
        ).reshape(-1, head_width)
    ).reshape(-1)
    gain_totals = []
    start = 0
    for n in gain_sizes:
        gain_totals.append(gain_rows[start : start + n])
        start += n
    return (
        pick_blocks(out_hidden, unorder)[None],
        pick_blocks(grad_inputs, unorder)[None],
        grad_query_w,
        grad_key_w,
        grad_value_w,
        grad_out_w,
        grad_gate_w,
        grad_up_w,
        grad_down_w,
        gain_totals[0],
        gain_totals[1],
        gain_totals[2],
        gain_totals[3],
    )


def solution(mesh):
    placed = (
        P("seq", "ctx", None),
        P("seq", "ctx"),
        P(),
        P(("seq", "ctx"), None),
        P(("seq", "ctx"), None),
        P(("seq", "ctx"), None),
        P(),
        P(),
        P(("seq", "ctx"), None),
        P(),
        P(("seq", "ctx"), None),
        P(("seq", "ctx"), None),
        P(("seq", "ctx"), None),
        P("seq", "ctx", None),
    )
    layer = sliced_layer if can_slice(mesh) else gathered_layer
    return jax.shard_map(
        layer,
        mesh=mesh,
        in_specs=placed,
        out_specs=(
            P("seq", "ctx", None),
            P("seq", "ctx", None),
            P(("seq", "ctx"), None),
            P(("seq", "ctx"), None),
            P(("seq", "ctx"), None),
            P(("seq", "ctx"), None),
            P(("seq", "ctx"), None),
            P(("seq", "ctx"), None),
            P(("seq", "ctx"), None),
            P(),
            P(),
            P(),
            P(),
        ),
        check_vma=False,
    )
```

```python
import functools

import jax
import jax.numpy as jnp
from jax import lax
from jax.experimental import pallas as pl
from jax.experimental.pallas import tpu as pltpu
from jax.sharding import PartitionSpec as P


NORM_EPSILON = 1e-06
ROPE_THETA = 1000000.0


def rope_tables(position_ids, head_width):
    half_width = head_width // 2
    inverse = ROPE_THETA ** (-(2.0 / head_width) * jnp.arange(half_width, dtype=jnp.float32))
    angles = position_ids.astype(jnp.float32)[:, None] * inverse[None, :]
    return (jnp.cos(angles), jnp.sin(angles))


def rotate(vectors, cosine, sine):
    half_width = vectors.shape[-1] // 2
    first = vectors[..., :half_width]
    second = vectors[..., half_width:]
    cos_rows = cosine[:, None, :]
    sin_rows = sine[:, None, :]
    return jnp.concatenate(
        (first * cos_rows - second * sin_rows, second * cos_rows + first * sin_rows), -1
    )


def rotate_back(grads, cosine, sine):
    half_width = grads.shape[-1] // 2
    first = grads[..., :half_width]
    second = grads[..., half_width:]
    cos_rows = cosine[:, None, :]
    sin_rows = sine[:, None, :]
    return jnp.concatenate(
        (first * cos_rows + second * sin_rows, second * cos_rows - first * sin_rows), -1
    )


def unit_rows(vectors):
    factor = lax.rsqrt(jnp.mean(vectors * vectors, -1, keepdims=True) + NORM_EPSILON)
    return (factor, vectors * factor)


def unit_back(grad_unit, factor, unit):
    return factor * (grad_unit - unit * jnp.mean(grad_unit * unit, -1, keepdims=True))


def outer_rows(left, right):
    return jnp.einsum("tj,tc->jc", left, right, preferred_element_type=jnp.float32)


def gathered_layer(
    hidden_in,
    positions,
    norm1_gain,
    w_query,
    key_weight_matrix,
    value_weight_matrix,
    query_gain,
    key_gain,
    w_out,
    norm2_gain,
    w_gate,
    w_up,
    w_down,
    cotangent,
):
    row_count = hidden_in.shape[1]
    head_width = query_gain.shape[0]
    query_columns = w_query.shape[1]
    key_value_columns = key_weight_matrix.shape[1]
    kv_heads = key_value_columns // head_width
    query_group_count = query_columns // key_value_columns
    attn_width = query_columns + 2 * key_value_columns + query_columns
    inputs = hidden_in[0].astype(jnp.float32)
    position_ids = positions[0]
    factor1, unit1 = unit_rows(inputs)
    normed1 = (unit1 * norm1_gain).astype(jnp.bfloat16)
    w_joint = jnp.concatenate((w_query, key_weight_matrix, value_weight_matrix), 1)
    joint_full, out_full = (
        lax.all_gather(w_joint, ("seq", "ctx"), axis=0, tiled=True),
        lax.all_gather(w_out, ("seq", "ctx"), axis=0, tiled=True),
    )
    projected_output = jnp.dot(normed1, joint_full, preferred_element_type=jnp.float32)
    query_raw = projected_output[:, :query_columns].reshape(
        row_count, query_columns // head_width, head_width
    )
    unrotated_key = projected_output[:, query_columns : query_columns + key_value_columns].reshape(
        row_count, kv_heads, head_width
    )
    unprojected_value = projected_output[:, query_columns + key_value_columns :].reshape(
        row_count, kv_heads, head_width
    )
    query_factor, query_unit = unit_rows(query_raw)
    key_factor, key_unit = unit_rows(unrotated_key)
    cosine, sine = rope_tables(position_ids, head_width)
    rotated_query = rotate(query_unit * query_gain, cosine, sine).astype(jnp.bfloat16)
    key_rot = rotate(key_unit * key_gain, cosine, sine).astype(jnp.bfloat16)
    query_head_rows = rotated_query.reshape(
        row_count, kv_heads, query_group_count, head_width
    ).transpose(1, 2, 0, 3)
    own_pair = jnp.stack((key_rot, unprojected_value.astype(jnp.bfloat16)))
    cycle_size = lax.axis_size("ctx")
    my_block = lax.axis_index("ctx")
    offsets = jnp.arange(row_count, dtype=jnp.int32)
    query_index = my_block * row_count + offsets
    doc_begin = query_index - position_ids
    score_scale = head_width ** (-0.5)

    def visible(count):
        key_index = jnp.arange(count, dtype=jnp.int32)
        return (key_index[None, :] <= query_index[:, None]) & (
            key_index[None, :] >= doc_begin[:, None]
        )

    def block_scores(key_value_couple, key_mask):
        scores = score_scale * jnp.einsum(
            "ekla,xea->eklx",
            query_head_rows,
            key_value_couple[0],
            preferred_element_type=jnp.float32,
        )
        return jnp.where(key_mask[None, None], scores, -jnp.inf)

    state = (
        jnp.full((kv_heads, query_group_count, row_count), -jnp.inf, jnp.float32),
        jnp.zeros((kv_heads, query_group_count, row_count), jnp.float32),
        jnp.zeros((kv_heads, query_group_count, row_count, head_width), jnp.float32),
    )
    key_value_couple = lax.all_gather(own_pair, "ctx", axis=1, tiled=True)
    key_mask = visible(key_value_couple.shape[1])

    def attend(current):
        highest, totals, accum = current
        scores = block_scores(key_value_couple, key_mask)
        new_high = jnp.max(scores, -1)
        decay = jnp.exp(highest - new_high)
        weights = jnp.exp(scores - new_high[..., None])
        totals = totals * decay + jnp.sum(weights, -1)
        accum = accum * decay[..., None] + jnp.einsum(
            "emaj,jep->emap",
            weights.astype(jnp.bfloat16),
            key_value_couple[1],
            preferred_element_type=jnp.float32,
        )
        return (new_high, totals, accum)

    highest, totals, accum = lax.cond(jnp.any(key_mask), attend, lambda current: current, state)
    log_total = highest + jnp.log(totals)
    attn_heads = (accum / totals[..., None]).astype(jnp.bfloat16)
    attention_row_block = attn_heads.transpose(2, 0, 1, 3).reshape(row_count, query_columns)
    attn_out = jnp.einsum(
        "tc,jc->tj", attention_row_block, out_full, preferred_element_type=jnp.float32
    )
    residual = inputs + attn_out
    factor2, unit2 = unit_rows(residual)
    normed2 = (unit2 * norm2_gain).astype(jnp.bfloat16)
    gate_full, up_full, down_full = (
        lax.all_gather(w_gate, ("seq", "ctx"), axis=0, tiled=True),
        lax.all_gather(w_up, ("seq", "ctx"), axis=0, tiled=True),
        lax.all_gather(w_down, ("seq", "ctx"), axis=0, tiled=True),
    )
    gate = jnp.dot(normed2, gate_full, preferred_element_type=jnp.float32)
    upward = jnp.dot(normed2, up_full, preferred_element_type=jnp.float32)
    sigmoid = jax.nn.sigmoid(gate)
    activation = gate * sigmoid
    hidden_units = (activation * upward).astype(jnp.bfloat16)
    mlp_out = jnp.einsum("tf,jf->tj", hidden_units, down_full, preferred_element_type=jnp.float32)
    out_hidden = (residual + mlp_out).astype(jnp.bfloat16)
    grad_out_b = cotangent[0]
    grad_hidden = jnp.dot(grad_out_b, down_full, preferred_element_type=jnp.float32)
    grad_gate = (grad_hidden * upward * sigmoid * (1.0 + gate * (1.0 - sigmoid))).astype(
        jnp.bfloat16
    )
    grad_up = (grad_hidden * activation).astype(jnp.bfloat16)
    grad_normed2 = jnp.einsum(
        "tf,jf->tj", grad_gate, gate_full, preferred_element_type=jnp.float32
    ) + jnp.einsum("tf,jf->tj", grad_up, up_full, preferred_element_type=jnp.float32)
    gain2_local = jnp.sum(grad_normed2 * unit2, 0)
    grad_residual = grad_out_b.astype(jnp.float32) + unit_back(
        grad_normed2 * norm2_gain, factor2, unit2
    )
    grad_residual_b = grad_residual.astype(jnp.bfloat16)
    grad_attn = jnp.dot(grad_residual_b, out_full, preferred_element_type=jnp.float32)
    attention_gradient_backward = grad_attn.astype(jnp.bfloat16)
    head_gradient = attention_gradient_backward.reshape(
        row_count, kv_heads, query_group_count, head_width
    ).transpose(1, 2, 0, 3)
    delta_rows = jnp.sum(head_gradient.astype(jnp.float32) * attn_heads.astype(jnp.float32), -1)
    grads_full = jnp.zeros((2, row_count * cycle_size, kv_heads, head_width), jnp.float32)
    grad_q_acc = jnp.zeros((kv_heads, query_group_count, row_count, head_width), jnp.float32)
    current = (grads_full, grad_q_acc)
    backward_key_value_couple = lax.all_gather(own_pair, "ctx", axis=1, tiled=True)
    piece_rows = backward_key_value_couple.shape[1]
    backward_key_mask = visible(piece_rows)

    def attend_back(inner):
        scores = block_scores(backward_key_value_couple, backward_key_mask)
        probs = jnp.exp(scores - log_total[..., None])
        probability_backward = probs.astype(jnp.bfloat16)
        grad_probs = jnp.einsum(
            "ekla,xea->eklx",
            head_gradient,
            backward_key_value_couple[1],
            preferred_element_type=jnp.float32,
        )
        score_gradient = (probs * (grad_probs - delta_rows[..., None])).astype(jnp.bfloat16)
        grad_q_acc = score_scale * jnp.einsum(
            "emaj,jep->emap",
            score_gradient,
            backward_key_value_couple[0],
            preferred_element_type=jnp.float32,
        )
        grad_keys = score_scale * jnp.einsum(
            "kejx,kejy->xky", score_gradient, query_head_rows, preferred_element_type=jnp.float32
        )
        grad_values = jnp.einsum(
            "kejx,kejy->xky",
            probability_backward,
            head_gradient,
            preferred_element_type=jnp.float32,
        )
        grads_full = jnp.stack((grad_keys, grad_values))
        return (grads_full, grad_q_acc)

    grads_full, grad_q_acc = lax.cond(
        jnp.any(backward_key_mask), attend_back, lambda inner: inner, current
    )
    grads_kv = lax.psum_scatter(
        grads_full.astype(jnp.bfloat16), "ctx", scatter_dimension=1, tiled=True
    ).astype(jnp.float32)
    grad_query = rotate_back(
        grad_q_acc.transpose(2, 0, 1, 3).reshape(
            row_count, query_columns // head_width, head_width
        ),
        cosine,
        sine,
    )
    grad_key = rotate_back(grads_kv[0], cosine, sine)
    qgain_local = jnp.sum(grad_query * query_unit, (0, 1))
    kgain_local = jnp.sum(grad_key * key_unit, (0, 1))
    grad_query_raw = unit_back(grad_query * query_gain, query_factor, query_unit)
    grad_key_raw = unit_back(grad_key * key_gain, key_factor, key_unit)
    grad_joint = jnp.concatenate(
        (
            grad_query_raw.reshape(row_count, query_columns),
            grad_key_raw.reshape(row_count, key_value_columns),
            grads_kv[1].reshape(row_count, key_value_columns),
        ),
        1,
    ).astype(jnp.bfloat16)
    grad_normed1 = jnp.einsum(
        "tc,jc->tj", grad_joint, joint_full, preferred_element_type=jnp.float32
    )
    gain1_local = jnp.sum(grad_normed1 * unit1, 0)
    grad_inputs = (grad_residual + unit_back(grad_normed1 * norm1_gain, factor1, unit1)).astype(
        jnp.bfloat16
    )
    joined = lax.psum_scatter(
        jnp.concatenate(
            (
                jnp.concatenate(
                    (
                        outer_rows(normed1, grad_joint),
                        outer_rows(grad_residual_b, attention_row_block),
                    ),
                    1,
                ),
                jnp.concatenate(
                    (
                        outer_rows(normed2, grad_gate),
                        outer_rows(normed2, grad_up),
                        outer_rows(grad_out_b, hidden_units),
                    ),
                    1,
                ),
            ),
            1,
        ),
        ("seq", "ctx"),
        scatter_dimension=0,
        tiled=True,
    )
    attn_grads = joined[:, :attn_width]
    mlp_grads = joined[:, attn_width:]
    gain_totals = lax.psum((gain1_local, gain2_local, qgain_local, kgain_local), ("seq", "ctx"))
    hidden_width = w_gate.shape[1]
    return (
        out_hidden[None],
        grad_inputs[None],
        attn_grads[:, :query_columns],
        attn_grads[:, query_columns : query_columns + key_value_columns],
        attn_grads[:, query_columns + key_value_columns : query_columns + 2 * key_value_columns],
        attn_grads[:, query_columns + 2 * key_value_columns :],
        mlp_grads[:, :hidden_width],
        mlp_grads[:, hidden_width : 2 * hidden_width],
        mlp_grads[:, 2 * hidden_width :],
        gain_totals[0],
        gain_totals[1],
        gain_totals[2],
        gain_totals[3],
    )


def turn(rows, cosine, sine):
    return rows * cosine + pltpu.roll(rows, rows.shape[-1] // 2, 1) * sine


def head_rows(raw, gain, cosine, sine):
    factor, unit = unit_rows(raw)
    return factor, unit, turn(unit * gain, cosine, sine).astype(jnp.bfloat16)


def dot_of(left, right, left_dim, right_dim):
    return lax.dot_general(
        left, right, (((left_dim,), (right_dim,)), ((), ())), preferred_element_type=jnp.float32
    )


def probabilities(key_rot, query_rot, mask):
    scores = dot_of(key_rot, query_rot, 1, 1) * key_rot.shape[-1] ** (-0.5) + mask
    weights = jnp.exp(scores - jnp.max(scores, 0, keepdims=True))
    return weights / jnp.sum(weights, 0, keepdims=True)


def attend_kernel(group, width, q_ref, k_ref, v_ref, mask_ref, cos_ref, sin_ref, qg_ref, kg_ref, o_ref):
    cosine, sine = cos_ref[...], sin_ref[...]
    key_rot = head_rows(k_ref[...], kg_ref[...], cosine, sine)[2]
    value = v_ref[...].astype(jnp.bfloat16)
    for r in range(group):
        cols = slice(r * width, (r + 1) * width)
        query_rot = head_rows(q_ref[:, cols], qg_ref[...], cosine, sine)[2]
        probs = probabilities(key_rot, query_rot, mask_ref[...]).astype(jnp.bfloat16)
        o_ref[:, cols] = dot_of(value, probs, 0, 0).T.astype(jnp.bfloat16)


def attend_back_kernel(
    group, width, q_ref, k_ref, v_ref, attn_ref, grad_ref, mask_ref, cos_ref, sin_ref,
    qg_ref, kg_ref, d_ref, gain_ref,
):
    cosine, sine = cos_ref[...], sin_ref[...]
    scale = width ** (-0.5)
    here = pl.program_id(0)
    kv_heads = pl.num_programs(0)

    def columns(head):
        return pl.ds(pl.multiple_of(head * width, width), width)

    key_factor, key_unit, key_rot = head_rows(k_ref[...], kg_ref[...], cosine, sine)
    value = v_ref[...].astype(jnp.bfloat16)

    @pl.when(pl.program_id(0) == 0)
    def _():
        gain_ref[...] = jnp.zeros_like(gain_ref)

    grad_key = jnp.zeros(key_rot.shape, jnp.float32)
    grad_value = jnp.zeros(key_rot.shape, jnp.float32)
    for r in range(group):
        cols = slice(r * width, (r + 1) * width)
        query_factor, query_unit, query_rot = head_rows(q_ref[:, cols], qg_ref[...], cosine, sine)
        probs = probabilities(key_rot, query_rot, mask_ref[...])
        grad = grad_ref[:, cols]
        product = grad.astype(jnp.float32) * attn_ref[:, cols].astype(jnp.float32)
        delta = jnp.sum(product.T, 0, keepdims=True)
        grad_scores = (probs * (dot_of(value, grad, 1, 1) - delta)).astype(jnp.bfloat16)
        grad_value += dot_of(probs.astype(jnp.bfloat16), grad, 1, 0)
        grad_key += dot_of(grad_scores, query_rot, 1, 0)
        grad_query = turn(scale * dot_of(key_rot, grad_scores, 0, 0).T, cosine, -sine)
        gain_ref[0:1, :] += jnp.sum(grad_query * query_unit, 0, keepdims=True)
        grad_query = unit_back(grad_query * qg_ref[...], query_factor, query_unit)
        d_ref[:, columns(here * group + r)] = grad_query.astype(jnp.bfloat16)
    grad_key = turn(scale * grad_key, cosine, -sine)
    gain_ref[1:2, :] += jnp.sum(grad_key * key_unit, 0, keepdims=True)
    grad_key = unit_back(grad_key * kg_ref[...], key_factor, key_unit)
    d_ref[:, columns(kv_heads * group + here)] = grad_key.astype(jnp.bfloat16)
    d_ref[:, columns(kv_heads * (group + 1) + here)] = grad_value.astype(jnp.bfloat16)


def attend_specs(tokens, width, heads, kv_heads):
    group = heads // kv_heads
    query = pl.BlockSpec((tokens, group * width), lambda h: (0, h))
    key = pl.BlockSpec((tokens, width), lambda h: (0, heads + h))
    value = pl.BlockSpec((tokens, width), lambda h: (0, heads + kv_heads + h))
    square = pl.BlockSpec((tokens, tokens), lambda h: (0, 0))
    table = pl.BlockSpec((tokens, width), lambda h: (0, 0))
    gain = pl.BlockSpec((1, width), lambda h: (0, 0))
    return query, key, value, square, table, gain


def attend(projected, mask, cosine, sine, gains, heads, kv_heads):
    tokens, width = cosine.shape
    query, key, value, square, table, gain = attend_specs(tokens, width, heads, kv_heads)
    return pl.pallas_call(
        functools.partial(attend_kernel, heads // kv_heads, width),
        grid=(kv_heads,),
        in_specs=[query, key, value, square, table, table, gain, gain],
        out_specs=query,
        out_shape=jax.ShapeDtypeStruct((tokens, heads * width), jnp.bfloat16),
        compiler_params=pltpu.CompilerParams(vmem_limit_bytes=16 << 20),
        name="attend",
    )(projected, projected, projected, mask, cosine, sine, *gains)


def attend_back(projected, attn, grad_attn, mask, cosine, sine, gains, heads, kv_heads):
    tokens, width = cosine.shape
    query, key, value, square, table, gain = attend_specs(tokens, width, heads, kv_heads)
    return pl.pallas_call(
        functools.partial(attend_back_kernel, heads // kv_heads, width),
        grid=(kv_heads,),
        in_specs=[query, key, value, query, query, square, table, table, gain, gain],
        out_specs=[
            pl.BlockSpec(projected.shape, lambda h: (0, 0)),
            pl.BlockSpec((8, width), lambda h: (0, 0)),
        ],
        out_shape=[
            jax.ShapeDtypeStruct(projected.shape, jnp.bfloat16),
            jax.ShapeDtypeStruct((8, width), jnp.float32),
        ],
        compiler_params=pltpu.CompilerParams(vmem_limit_bytes=24 << 20),
        name="attend_back",
    )(projected, projected, projected, attn, grad_attn, mask, cosine, sine, *gains)


def pack_kernel(count, *refs):
    matrices, out, sems = refs[:-2], refs[-2], refs[-1]
    copies = []
    start = 0
    for k, matrix in enumerate(matrices):
        n = matrix.shape[1] // count
        for d in range(count):
            copies.append(
                pltpu.make_async_copy(
                    matrix.at[:, d * n : (d + 1) * n],
                    out.at[d, :, start : start + n],
                    sems.at[k, d],
                )
            )
        start += n
    for copy in copies:
        copy.start()
    for copy in copies:
        copy.wait()


def pack(matrices, count):
    rows = matrices[0].shape[0]
    cols = sum(m.shape[1] for m in matrices) // count
    anywhere = pl.BlockSpec(memory_space=pl.ANY)
    return pl.pallas_call(
        functools.partial(pack_kernel, count),
        in_specs=[pl.BlockSpec(memory_space=pltpu.HBM)] * len(matrices),
        out_specs=anywhere,
        out_shape=jax.ShapeDtypeStruct((count, rows, cols), matrices[0].dtype),
        scratch_shapes=[pltpu.SemaphoreType.DMA((len(matrices), count))],
        name="pack",
    )(*matrices)


def unpack_kernel(sizes, pieces_ref, *outs):
    start = 0
    for out, n in zip(outs, sizes):
        for d in range(pieces_ref.shape[0]):
            piece = pieces_ref[d, :, start : start + n]
            out[:, d * n : (d + 1) * n] = piece.astype(jnp.float32)
        start += n


def unpack(pieces, sizes):
    count, rows, _ = pieces.shape
    return pl.pallas_call(
        functools.partial(unpack_kernel, tuple(sizes)),
        out_shape=[jax.ShapeDtypeStruct((rows, count * n), jnp.float32) for n in sizes],
        compiler_params=pltpu.CompilerParams(vmem_limit_bytes=8 << 20),
        name="unpack",
    )(pieces)


def can_slice(mesh):
    seq_size = mesh.shape["seq"]
    ctx_size = mesh.shape["ctx"]
    return seq_size == 8 and ctx_size == 4


def swap_ctx(array, bit, seq_size, ctx_size):
    pairs = [
        (s * ctx_size + c, s * ctx_size + (c ^ bit))
        for s in range(seq_size)
        for c in range(ctx_size)
    ]
    return lax.ppermute(array, ("seq", "ctx"), pairs)


def sliced_layer(*arrays):
    return sliced_body(*arrays)


def sliced_body(
    hidden_in,
    positions,
    norm1_gain,
    w_query,
    key_weight_matrix,
    value_weight_matrix,
    query_gain,
    key_gain,
    w_out,
    norm2_gain,
    w_gate,
    w_up,
    w_down,
    cotangent,
):
    seq_size = lax.axis_size("seq")
    ctx_size = lax.axis_size("ctx")
    my_seq = lax.axis_index("seq")
    my_ctx = lax.axis_index("ctx")
    row_count = hidden_in.shape[1]
    width = hidden_in.shape[2]
    head_width = query_gain.shape[0]
    heads = w_query.shape[1] // head_width // ctx_size
    kv_heads = key_weight_matrix.shape[1] // head_width // ctx_size
    hidden_cols = w_gate.shape[1] // ctx_size
    bits = [1 << b for b in reversed(range(ctx_size.bit_length() - 1))]
    block = width // seq_size
    half = seq_size // 2

    def spot_of(s):
        return jnp.where(s % 2 == 0, s // 2, seq_size - 1 - s // 2)

    ring = list(range(0, seq_size, 2)) + list(range(seq_size - 1, 0, -2))
    spot = spot_of(my_seq)
    offsets = [0]
    for k in range(1, half):
        offsets += [-k, k]
    offsets.append(half)
    place = {o % seq_size: k for k, o in enumerate(offsets)}
    order = []
    for o in offsets:
        r = (spot + (o + seq_size)) % seq_size
        order.append(jnp.where(r < half, 2 * r, 2 * (seq_size - 1 - r) + 1))
    unorder = []
    for s in range(seq_size):
        r = (ring.index(s) + seq_size - spot) % seq_size
        near = jnp.where(r < half, 2 * r, 2 * (seq_size - r) - 1)
        unorder.append(jnp.where(r == half, seq_size - 1, near))

    def pick_blocks(array, which):
        return jnp.concatenate(
            [
                lax.dynamic_slice_in_dim(array, which[k] * block, block, array.ndim - 1)
                for k in range(seq_size)
            ],
            array.ndim - 1,
        )

    def shift(array, by):
        pairs = [
            (
                ring[r] * ctx_size + c,
                ring[(r + by) % seq_size] * ctx_size + c,
            )
            for r in range(seq_size)
            for c in range(ctx_size)
        ]
        return lax.ppermute(array, ("seq", "ctx"), pairs)

    def swap(array, bit):
        return swap_ctx(array, bit, seq_size, ctx_size)

    def exchange(pieces):
        rest = pieces.shape[1:]
        state = pieces.reshape((2,) * len(bits) + rest)
        for axis, bit in enumerate(bits):
            mine = (my_ctx & bit) != 0
            low = lax.index_in_dim(state, 0, axis, False)
            high = lax.index_in_dim(state, 1, axis, False)
            keep = jnp.where(mine, high, low)
            got = swap(jnp.where(mine, low, high), bit)
            source = lax.broadcasted_iota(jnp.int32, state.shape, axis) == mine.astype(jnp.int32)
            state = jnp.where(source, jnp.expand_dims(keep, axis), jnp.expand_dims(got, axis))
        return state.reshape((ctx_size,) + rest)

    def join_tokens(array):
        for bit in bits:
            array = jnp.concatenate((array, swap(array, bit)), 0)
        return array

    def sum_tokens(array):
        for bit in reversed(bits):
            rows = array.shape[0] // 2
            got = swap(array[rows:].astype(jnp.bfloat16), bit)
            array = array[:rows] + got.astype(jnp.float32)
        return array

    def after(array, *others):
        return lax.optimization_barrier((array, *others))[0] if others else array

    def gather_rows(own, gates):
        blocks = [own]
        ahead = back = own
        for k in range(1, half):
            ahead = shift(ahead, 1)
            back = shift(back, -1)
            ahead, back = lax.optimization_barrier((ahead, back) + tuple(gates.get(k, ())))[:2]
            blocks += [ahead, back]
        middle = block // 2
        ahead = shift(ahead[:middle], 1)
        back = shift(back[middle:], -1)
        blocks.append(jnp.concatenate((ahead, back), 0))
        return blocks

    def scatter_rows(pairs):
        def rows_of(offset, sent):
            k = place[offset % seq_size]
            return jnp.concatenate(
                [dot(x[:, k * block : (k + 1) * block], after(g, *sent), first) for x, g in pairs],
                1,
            )

        middle = block // 2
        far = rows_of(half, ()).astype(jnp.bfloat16)
        sends = [(far[:middle], far[middle:])]
        for k in range(half - 1, -1, -1):
            ahead = shift(sends[-1][0], 1).astype(jnp.float32)
            back = shift(sends[-1][1], -1).astype(jnp.float32)
            if k == 0:
                total = rows_of(0, sends[-1]) + ahead + back
                return total.astype(jnp.bfloat16), sends
            to_ahead = rows_of(k, sends[-1])
            to_back = rows_of(-k, sends[-1])
            if k == half - 1:
                to_ahead = jnp.concatenate((to_ahead[:middle] + ahead, to_ahead[middle:]), 0)
                to_back = jnp.concatenate((to_back[:middle], to_back[middle:] + back), 0)
            else:
                to_ahead = to_ahead + ahead
                to_back = to_back + back
            sends.append(
                lax.optimization_barrier(
                    (to_ahead.astype(jnp.bfloat16), to_back.astype(jnp.bfloat16))
                )
            )

    def own_rows(matrices):
        return exchange(pack(matrices, ctx_size)).reshape(block, -1)

    def sum_all(array):
        for bit in reversed(bits):
            array = array + swap(array, bit)
        bit = 1
        while bit < seq_size:
            pairs = [
                (s * ctx_size + c, (s ^ bit) * ctx_size + c)
                for s in range(seq_size)
                for c in range(ctx_size)
            ]
            array = array + lax.ppermute(array, ("seq", "ctx"), pairs)
            bit *= 2
        return array

    def collect(rows, sizes):
        pieces = exchange(rows.reshape(ctx_size, -1, rows.shape[1]))
        return unpack(pieces, sizes)

    def dot(left, right, dims):
        return lax.dot_general(left, right, (dims, ((), ())), preferred_element_type=jnp.float32)

    plain = ((1,), (0,))
    last = ((1,), (1,))
    first = ((0,), (0,))

    gain1 = pick_blocks(norm1_gain, order)
    gain2 = pick_blocks(norm2_gain, order)
    inputs = pick_blocks(hidden_in[0], order).astype(jnp.float32)
    cot_own = pick_blocks(cotangent[0], order)
    factor1, unit1 = unit_rows(inputs)
    digits = jnp.where(
        jnp.arange(head_width)[None, :] < head_width // 2,
        positions[0][:, None] // 128,
        positions[0][:, None] % 128,
    ).astype(jnp.bfloat16)
    attn_own = own_rows([w_query, key_weight_matrix, value_weight_matrix, w_out])
    mlp_own = own_rows([w_gate, w_up, w_down])
    joined = join_tokens(
        jnp.concatenate(
            ((unit1 * gain1).astype(jnp.bfloat16), cot_own, digits), 1
        ),
    )
    normed1 = joined[:, :width]
    cot = joined[:, width : 2 * width]
    digits = joined[:, 2 * width :].astype(jnp.float32)
    position_ids = (digits[:, 0] * 128.0 + digits[:, head_width // 2]).astype(jnp.int32)

    query_cols = heads * head_width
    kv_cols = kv_heads * head_width
    owners = [0]
    for bit in bits:
        owners = owners + [o ^ bit for o in owners]
    index = jnp.concatenate(
        [(my_ctx ^ o) * row_count + jnp.arange(row_count, dtype=jnp.int32) for o in owners]
    )
    begin = index - position_ids
    allowed = (index[:, None] <= index[None, :]) & (index[:, None] >= begin[None, :])
    mask = jnp.where(allowed, 0.0, -jnp.inf)
    cosine, sine = rope_tables(position_ids, head_width)
    cosine = jnp.concatenate((cosine, cosine), 1)
    sine = jnp.concatenate((-sine, sine), 1)

    attn_blocks = gather_rows(attn_own, {half - 1: (mask, cosine, sine)})
    mlp_blocks = gather_rows(mlp_own, {})
    attn_full = jnp.concatenate(attn_blocks, 0)
    mlp_full = jnp.concatenate(mlp_blocks, 0)
    joint = attn_full[:, : query_cols + 2 * kv_cols]
    out_cols = attn_full[:, query_cols + 2 * kv_cols :]
    gate_up = mlp_full[:, : 2 * hidden_cols]
    down = mlp_full[:, 2 * hidden_cols :]

    projected = dot(normed1, joint, plain)
    gains = (query_gain[None, :], key_gain[None, :])
    attn = attend(projected, mask, cosine, sine, gains, heads, kv_heads)

    residual = inputs + sum_tokens(dot(attn, out_cols, last))
    factor2, unit2 = unit_rows(residual)
    normed2 = join_tokens((unit2 * gain2).astype(jnp.bfloat16))
    gate_up_out = dot(normed2, gate_up, plain)
    gate = gate_up_out[:, :hidden_cols]
    upward = gate_up_out[:, hidden_cols:]
    sigmoid = jax.nn.sigmoid(gate)
    activation = gate * sigmoid
    hidden_units = (activation * upward).astype(jnp.bfloat16)
    grad_hid = dot(cot, down, plain)
    grad_gate = grad_hid * upward * sigmoid * (1.0 + gate * (1.0 - sigmoid))
    grad_up = grad_hid * activation
    grad_gate_up = jnp.concatenate((grad_gate, grad_up), 1).astype(jnp.bfloat16)
    back_mlp = dot(grad_gate_up, gate_up, last)
    grad_normed2 = sum_tokens(back_mlp)
    gain2_local = jnp.sum(grad_normed2 * unit2, 0)
    grad_residual = cot_own.astype(jnp.float32) + unit_back(grad_normed2 * gain2, factor2, unit2)
    grad_residual_b = join_tokens(grad_residual.astype(jnp.bfloat16))
    grad_attn = dot(grad_residual_b, out_cols, plain).astype(jnp.bfloat16)
    mlp_rows, _ = scatter_rows([(cot, hidden_units), (normed2, grad_gate_up)])
    grad_joint, gain_local = attend_back(
        projected, attn, grad_attn, mask, cosine, sine, gains, heads, kv_heads
    )
    grad_down_w, grad_gate_w, grad_up_w = collect(mlp_rows, [hidden_cols] * 3)
    attn_rows, sends = scatter_rows([(grad_residual_b, attn), (normed1, grad_joint)])
    grad_out_w, grad_query_w, grad_key_w, grad_value_w = collect(
        attn_rows, [query_cols, query_cols, kv_cols, kv_cols]
    )
    late_units = after(hidden_units, *sends[2])
    late_out = dot(late_units, down, last)
    out_hidden = (residual + sum_tokens(late_out)).astype(jnp.bfloat16)

    back_joint = dot(grad_joint, joint, last)
    grad_normed1 = sum_tokens(back_joint)
    gain1_local = jnp.sum(grad_normed1 * unit1, 0)
    grad_inputs = (grad_residual + unit_back(grad_normed1 * gain1, factor1, unit1)).astype(
        jnp.bfloat16
    )
    gain_sizes = [width, width, head_width, head_width]
    gain_rows = sum_all(
        jnp.concatenate(
            (
                pick_blocks(gain1_local, unorder),
                pick_blocks(gain2_local, unorder),
                gain_local[0],
                gain_local[1],
            )
        ).reshape(-1, head_width),
    ).reshape(-1)
    gain_totals = []
    start = 0
    for n in gain_sizes:
        gain_totals.append(gain_rows[start : start + n])
        start += n
    return (
        pick_blocks(out_hidden, unorder)[None],
        pick_blocks(grad_inputs, unorder)[None],
        grad_query_w,
        grad_key_w,
        grad_value_w,
        grad_out_w,
        grad_gate_w,
        grad_up_w,
        grad_down_w,
        gain_totals[0],
        gain_totals[1],
        gain_totals[2],
        gain_totals[3],
    )


def solution(mesh):
    placed = (
        P("seq", "ctx", None),
        P("seq", "ctx"),
        P(),
        P(("seq", "ctx"), None),
        P(("seq", "ctx"), None),
        P(("seq", "ctx"), None),
        P(),
        P(),
        P(("seq", "ctx"), None),
        P(),
        P(("seq", "ctx"), None),
        P(("seq", "ctx"), None),
        P(("seq", "ctx"), None),
        P("seq", "ctx", None),
    )
    layer = sliced_layer if can_slice(mesh) else gathered_layer
    return jax.shard_map(
        layer,
        mesh=mesh,
        in_specs=placed,
        out_specs=(
            P("seq", "ctx", None),
            P("seq", "ctx", None),
            P(("seq", "ctx"), None),
            P(("seq", "ctx"), None),
            P(("seq", "ctx"), None),
            P(("seq", "ctx"), None),
            P(("seq", "ctx"), None),
            P(("seq", "ctx"), None),
            P(("seq", "ctx"), None),
            P(),
            P(),
            P(),
            P(),
        ),
        check_vma=False,
    )
```

```python
import functools

import jax
import jax.numpy as jnp
from jax import lax
from jax.experimental import pallas as pl
from jax.experimental.pallas import tpu as pltpu
from jax.sharding import PartitionSpec as P


NORM_EPSILON = 1e-06
ROPE_THETA = 1000000.0


def rope_tables(position_ids, head_width):
    half_width = head_width // 2
    inverse = ROPE_THETA ** (-(2.0 / head_width) * jnp.arange(half_width, dtype=jnp.float32))
    angles = position_ids.astype(jnp.float32)[:, None] * inverse[None, :]
    return (jnp.cos(angles), jnp.sin(angles))


def rotate(vectors, cosine, sine):
    half_width = vectors.shape[-1] // 2
    first = vectors[..., :half_width]
    second = vectors[..., half_width:]
    cos_rows = cosine[:, None, :]
    sin_rows = sine[:, None, :]
    return jnp.concatenate(
        (first * cos_rows - second * sin_rows, second * cos_rows + first * sin_rows), -1
    )


def rotate_back(grads, cosine, sine):
    half_width = grads.shape[-1] // 2
    first = grads[..., :half_width]
    second = grads[..., half_width:]
    cos_rows = cosine[:, None, :]
    sin_rows = sine[:, None, :]
    return jnp.concatenate(
        (first * cos_rows + second * sin_rows, second * cos_rows - first * sin_rows), -1
    )


def unit_rows(vectors):
    factor = lax.rsqrt(jnp.mean(vectors * vectors, -1, keepdims=True) + NORM_EPSILON)
    return (factor, vectors * factor)


def unit_back(grad_unit, factor, unit):
    return factor * (grad_unit - unit * jnp.mean(grad_unit * unit, -1, keepdims=True))


def outer_rows(left, right):
    return jnp.einsum("tj,tc->jc", left, right, preferred_element_type=jnp.float32)


def gathered_layer(
    hidden_in,
    positions,
    norm1_gain,
    w_query,
    key_weight_matrix,
    value_weight_matrix,
    query_gain,
    key_gain,
    w_out,
    norm2_gain,
    w_gate,
    w_up,
    w_down,
    cotangent,
):
    row_count = hidden_in.shape[1]
    head_width = query_gain.shape[0]
    query_columns = w_query.shape[1]
    key_value_columns = key_weight_matrix.shape[1]
    kv_heads = key_value_columns // head_width
    query_group_count = query_columns // key_value_columns
    attn_width = query_columns + 2 * key_value_columns + query_columns
    inputs = hidden_in[0].astype(jnp.float32)
    position_ids = positions[0]
    factor1, unit1 = unit_rows(inputs)
    normed1 = (unit1 * norm1_gain).astype(jnp.bfloat16)
    w_joint = jnp.concatenate((w_query, key_weight_matrix, value_weight_matrix), 1)
    joint_full, out_full = (
        lax.all_gather(w_joint, ("seq", "ctx"), axis=0, tiled=True),
        lax.all_gather(w_out, ("seq", "ctx"), axis=0, tiled=True),
    )
    projected_output = jnp.dot(normed1, joint_full, preferred_element_type=jnp.float32)
    query_raw = projected_output[:, :query_columns].reshape(
        row_count, query_columns // head_width, head_width
    )
    unrotated_key = projected_output[:, query_columns : query_columns + key_value_columns].reshape(
        row_count, kv_heads, head_width
    )
    unprojected_value = projected_output[:, query_columns + key_value_columns :].reshape(
        row_count, kv_heads, head_width
    )
    query_factor, query_unit = unit_rows(query_raw)
    key_factor, key_unit = unit_rows(unrotated_key)
    cosine, sine = rope_tables(position_ids, head_width)
    rotated_query = rotate(query_unit * query_gain, cosine, sine).astype(jnp.bfloat16)
    key_rot = rotate(key_unit * key_gain, cosine, sine).astype(jnp.bfloat16)
    query_head_rows = rotated_query.reshape(
        row_count, kv_heads, query_group_count, head_width
    ).transpose(1, 2, 0, 3)
    own_pair = jnp.stack((key_rot, unprojected_value.astype(jnp.bfloat16)))
    cycle_size = lax.axis_size("ctx")
    my_block = lax.axis_index("ctx")
    offsets = jnp.arange(row_count, dtype=jnp.int32)
    query_index = my_block * row_count + offsets
    doc_begin = query_index - position_ids
    score_scale = head_width ** (-0.5)

    def visible(count):
        key_index = jnp.arange(count, dtype=jnp.int32)
        return (key_index[None, :] <= query_index[:, None]) & (
            key_index[None, :] >= doc_begin[:, None]
        )

    def block_scores(key_value_couple, key_mask):
        scores = score_scale * jnp.einsum(
            "ekla,xea->eklx",
            query_head_rows,
            key_value_couple[0],
            preferred_element_type=jnp.float32,
        )
        return jnp.where(key_mask[None, None], scores, -jnp.inf)

    state = (
        jnp.full((kv_heads, query_group_count, row_count), -jnp.inf, jnp.float32),
        jnp.zeros((kv_heads, query_group_count, row_count), jnp.float32),
        jnp.zeros((kv_heads, query_group_count, row_count, head_width), jnp.float32),
    )
    key_value_couple = lax.all_gather(own_pair, "ctx", axis=1, tiled=True)
    key_mask = visible(key_value_couple.shape[1])

    def attend(current):
        highest, totals, accum = current
        scores = block_scores(key_value_couple, key_mask)
        new_high = jnp.max(scores, -1)
        decay = jnp.exp(highest - new_high)
        weights = jnp.exp(scores - new_high[..., None])
        totals = totals * decay + jnp.sum(weights, -1)
        accum = accum * decay[..., None] + jnp.einsum(
            "emaj,jep->emap",
            weights.astype(jnp.bfloat16),
            key_value_couple[1],
            preferred_element_type=jnp.float32,
        )
        return (new_high, totals, accum)

    highest, totals, accum = lax.cond(jnp.any(key_mask), attend, lambda current: current, state)
    log_total = highest + jnp.log(totals)
    attn_heads = (accum / totals[..., None]).astype(jnp.bfloat16)
    attention_row_block = attn_heads.transpose(2, 0, 1, 3).reshape(row_count, query_columns)
    attn_out = jnp.einsum(
        "tc,jc->tj", attention_row_block, out_full, preferred_element_type=jnp.float32
    )
    residual = inputs + attn_out
    factor2, unit2 = unit_rows(residual)
    normed2 = (unit2 * norm2_gain).astype(jnp.bfloat16)
    gate_full, up_full, down_full = (
        lax.all_gather(w_gate, ("seq", "ctx"), axis=0, tiled=True),
        lax.all_gather(w_up, ("seq", "ctx"), axis=0, tiled=True),
        lax.all_gather(w_down, ("seq", "ctx"), axis=0, tiled=True),
    )
    gate = jnp.dot(normed2, gate_full, preferred_element_type=jnp.float32)
    upward = jnp.dot(normed2, up_full, preferred_element_type=jnp.float32)
    sigmoid = jax.nn.sigmoid(gate)
    activation = gate * sigmoid
    hidden_units = (activation * upward).astype(jnp.bfloat16)
    mlp_out = jnp.einsum("tf,jf->tj", hidden_units, down_full, preferred_element_type=jnp.float32)
    out_hidden = (residual + mlp_out).astype(jnp.bfloat16)
    grad_out_b = cotangent[0]
    grad_hidden = jnp.dot(grad_out_b, down_full, preferred_element_type=jnp.float32)
    grad_gate = (grad_hidden * upward * sigmoid * (1.0 + gate * (1.0 - sigmoid))).astype(
        jnp.bfloat16
    )
    grad_up = (grad_hidden * activation).astype(jnp.bfloat16)
    grad_normed2 = jnp.einsum(
        "tf,jf->tj", grad_gate, gate_full, preferred_element_type=jnp.float32
    ) + jnp.einsum("tf,jf->tj", grad_up, up_full, preferred_element_type=jnp.float32)
    gain2_local = jnp.sum(grad_normed2 * unit2, 0)
    grad_residual = grad_out_b.astype(jnp.float32) + unit_back(
        grad_normed2 * norm2_gain, factor2, unit2
    )
    grad_residual_b = grad_residual.astype(jnp.bfloat16)
    grad_attn = jnp.dot(grad_residual_b, out_full, preferred_element_type=jnp.float32)
    attention_gradient_backward = grad_attn.astype(jnp.bfloat16)
    head_gradient = attention_gradient_backward.reshape(
        row_count, kv_heads, query_group_count, head_width
    ).transpose(1, 2, 0, 3)
    delta_rows = jnp.sum(head_gradient.astype(jnp.float32) * attn_heads.astype(jnp.float32), -1)
    grads_full = jnp.zeros((2, row_count * cycle_size, kv_heads, head_width), jnp.float32)
    grad_q_acc = jnp.zeros((kv_heads, query_group_count, row_count, head_width), jnp.float32)
    current = (grads_full, grad_q_acc)
    backward_key_value_couple = lax.all_gather(own_pair, "ctx", axis=1, tiled=True)
    piece_rows = backward_key_value_couple.shape[1]
    backward_key_mask = visible(piece_rows)

    def attend_back(inner):
        scores = block_scores(backward_key_value_couple, backward_key_mask)
        probs = jnp.exp(scores - log_total[..., None])
        probability_backward = probs.astype(jnp.bfloat16)
        grad_probs = jnp.einsum(
            "ekla,xea->eklx",
            head_gradient,
            backward_key_value_couple[1],
            preferred_element_type=jnp.float32,
        )
        score_gradient = (probs * (grad_probs - delta_rows[..., None])).astype(jnp.bfloat16)
        grad_q_acc = score_scale * jnp.einsum(
            "emaj,jep->emap",
            score_gradient,
            backward_key_value_couple[0],
            preferred_element_type=jnp.float32,
        )
        grad_keys = score_scale * jnp.einsum(
            "kejx,kejy->xky", score_gradient, query_head_rows, preferred_element_type=jnp.float32
        )
        grad_values = jnp.einsum(
            "kejx,kejy->xky",
            probability_backward,
            head_gradient,
            preferred_element_type=jnp.float32,
        )
        grads_full = jnp.stack((grad_keys, grad_values))
        return (grads_full, grad_q_acc)

    grads_full, grad_q_acc = lax.cond(
        jnp.any(backward_key_mask), attend_back, lambda inner: inner, current
    )
    grads_kv = lax.psum_scatter(
        grads_full.astype(jnp.bfloat16), "ctx", scatter_dimension=1, tiled=True
    ).astype(jnp.float32)
    grad_query = rotate_back(
        grad_q_acc.transpose(2, 0, 1, 3).reshape(
            row_count, query_columns // head_width, head_width
        ),
        cosine,
        sine,
    )
    grad_key = rotate_back(grads_kv[0], cosine, sine)
    qgain_local = jnp.sum(grad_query * query_unit, (0, 1))
    kgain_local = jnp.sum(grad_key * key_unit, (0, 1))
    grad_query_raw = unit_back(grad_query * query_gain, query_factor, query_unit)
    grad_key_raw = unit_back(grad_key * key_gain, key_factor, key_unit)
    grad_joint = jnp.concatenate(
        (
            grad_query_raw.reshape(row_count, query_columns),
            grad_key_raw.reshape(row_count, key_value_columns),
            grads_kv[1].reshape(row_count, key_value_columns),
        ),
        1,
    ).astype(jnp.bfloat16)
    grad_normed1 = jnp.einsum(
        "tc,jc->tj", grad_joint, joint_full, preferred_element_type=jnp.float32
    )
    gain1_local = jnp.sum(grad_normed1 * unit1, 0)
    grad_inputs = (grad_residual + unit_back(grad_normed1 * norm1_gain, factor1, unit1)).astype(
        jnp.bfloat16
    )
    joined = lax.psum_scatter(
        jnp.concatenate(
            (
                jnp.concatenate(
                    (
                        outer_rows(normed1, grad_joint),
                        outer_rows(grad_residual_b, attention_row_block),
                    ),
                    1,
                ),
                jnp.concatenate(
                    (
                        outer_rows(normed2, grad_gate),
                        outer_rows(normed2, grad_up),
                        outer_rows(grad_out_b, hidden_units),
                    ),
                    1,
                ),
            ),
            1,
        ),
        ("seq", "ctx"),
        scatter_dimension=0,
        tiled=True,
    )
    attn_grads = joined[:, :attn_width]
    mlp_grads = joined[:, attn_width:]
    gain_totals = lax.psum((gain1_local, gain2_local, qgain_local, kgain_local), ("seq", "ctx"))
    hidden_width = w_gate.shape[1]
    return (
        out_hidden[None],
        grad_inputs[None],
        attn_grads[:, :query_columns],
        attn_grads[:, query_columns : query_columns + key_value_columns],
        attn_grads[:, query_columns + key_value_columns : query_columns + 2 * key_value_columns],
        attn_grads[:, query_columns + 2 * key_value_columns :],
        mlp_grads[:, :hidden_width],
        mlp_grads[:, hidden_width : 2 * hidden_width],
        mlp_grads[:, 2 * hidden_width :],
        gain_totals[0],
        gain_totals[1],
        gain_totals[2],
        gain_totals[3],
    )


def turn(rows, cosine, sine):
    return rows * cosine + pltpu.roll(rows, rows.shape[-1] // 2, 1) * sine


def head_rows(raw, gain, cosine, sine):
    factor, unit = unit_rows(raw)
    return factor, unit, turn(unit * gain, cosine, sine).astype(jnp.bfloat16)


def dot_of(left, right, left_dim, right_dim):
    return lax.dot_general(
        left, right, (((left_dim,), (right_dim,)), ((), ())), preferred_element_type=jnp.float32
    )


def probabilities(key_rot, query_rot, mask):
    scores = dot_of(key_rot, query_rot, 1, 1) * key_rot.shape[-1] ** (-0.5) + mask
    weights = jnp.exp(scores - jnp.max(scores, 0, keepdims=True))
    return weights / jnp.sum(weights, 0, keepdims=True)


def attend_kernel(group, width, q_ref, k_ref, v_ref, mask_ref, cos_ref, sin_ref, qg_ref, kg_ref, o_ref):
    cosine, sine = cos_ref[...], sin_ref[...]
    key_rot = head_rows(k_ref[...], kg_ref[...], cosine, sine)[2]
    value = v_ref[...].astype(jnp.bfloat16)
    for r in range(group):
        cols = slice(r * width, (r + 1) * width)
        query_rot = head_rows(q_ref[:, cols], qg_ref[...], cosine, sine)[2]
        probs = probabilities(key_rot, query_rot, mask_ref[...]).astype(jnp.bfloat16)
        o_ref[:, cols] = dot_of(value, probs, 0, 0).T.astype(jnp.bfloat16)


def attend_back_kernel(
    group, width, q_ref, k_ref, v_ref, attn_ref, grad_ref, mask_ref, cos_ref, sin_ref,
    qg_ref, kg_ref, d_ref, gain_ref,
):
    cosine, sine = cos_ref[...], sin_ref[...]
    scale = width ** (-0.5)
    here = pl.program_id(0)
    kv_heads = pl.num_programs(0)

    def columns(head):
        return pl.ds(pl.multiple_of(head * width, width), width)

    key_factor, key_unit, key_rot = head_rows(k_ref[...], kg_ref[...], cosine, sine)
    value = v_ref[...].astype(jnp.bfloat16)

    @pl.when(pl.program_id(0) == 0)
    def _():
        gain_ref[...] = jnp.zeros_like(gain_ref)

    grad_key = jnp.zeros(key_rot.shape, jnp.float32)
    grad_value = jnp.zeros(key_rot.shape, jnp.float32)
    for r in range(group):
        cols = slice(r * width, (r + 1) * width)
        query_factor, query_unit, query_rot = head_rows(q_ref[:, cols], qg_ref[...], cosine, sine)
        probs = probabilities(key_rot, query_rot, mask_ref[...])
        grad = grad_ref[:, cols]
        product = grad.astype(jnp.float32) * attn_ref[:, cols].astype(jnp.float32)
        delta = jnp.sum(product.T, 0, keepdims=True)
        grad_scores = (probs * (dot_of(value, grad, 1, 1) - delta)).astype(jnp.bfloat16)
        grad_value += dot_of(probs.astype(jnp.bfloat16), grad, 1, 0)
        grad_key += dot_of(grad_scores, query_rot, 1, 0)
        grad_query = turn(scale * dot_of(key_rot, grad_scores, 0, 0).T, cosine, -sine)
        gain_ref[0:1, :] += jnp.sum(grad_query * query_unit, 0, keepdims=True)
        grad_query = unit_back(grad_query * qg_ref[...], query_factor, query_unit)
        d_ref[:, columns(here * group + r)] = grad_query.astype(jnp.bfloat16)
    grad_key = turn(scale * grad_key, cosine, -sine)
    gain_ref[1:2, :] += jnp.sum(grad_key * key_unit, 0, keepdims=True)
    grad_key = unit_back(grad_key * kg_ref[...], key_factor, key_unit)
    d_ref[:, columns(kv_heads * group + here)] = grad_key.astype(jnp.bfloat16)
    d_ref[:, columns(kv_heads * (group + 1) + here)] = grad_value.astype(jnp.bfloat16)


def attend_specs(tokens, width, heads, kv_heads):
    group = heads // kv_heads
    query = pl.BlockSpec((tokens, group * width), lambda h: (0, h))
    key = pl.BlockSpec((tokens, width), lambda h: (0, heads + h))
    value = pl.BlockSpec((tokens, width), lambda h: (0, heads + kv_heads + h))
    square = pl.BlockSpec((tokens, tokens), lambda h: (0, 0))
    table = pl.BlockSpec((tokens, width), lambda h: (0, 0))
    gain = pl.BlockSpec((1, width), lambda h: (0, 0))
    return query, key, value, square, table, gain


def attend(projected, mask, cosine, sine, gains, heads, kv_heads):
    tokens, width = cosine.shape
    query, key, value, square, table, gain = attend_specs(tokens, width, heads, kv_heads)
    return pl.pallas_call(
        functools.partial(attend_kernel, heads // kv_heads, width),
        grid=(kv_heads,),
        in_specs=[query, key, value, square, table, table, gain, gain],
        out_specs=query,
        out_shape=jax.ShapeDtypeStruct((tokens, heads * width), jnp.bfloat16),
        compiler_params=pltpu.CompilerParams(vmem_limit_bytes=16 << 20),
        name="attend",
    )(projected, projected, projected, mask, cosine, sine, *gains)


def attend_back(projected, attn, grad_attn, mask, cosine, sine, gains, heads, kv_heads):
    tokens, width = cosine.shape
    query, key, value, square, table, gain = attend_specs(tokens, width, heads, kv_heads)
    return pl.pallas_call(
        functools.partial(attend_back_kernel, heads // kv_heads, width),
        grid=(kv_heads,),
        in_specs=[query, key, value, query, query, square, table, table, gain, gain],
        out_specs=[
            pl.BlockSpec(projected.shape, lambda h: (0, 0)),
            pl.BlockSpec((8, width), lambda h: (0, 0)),
        ],
        out_shape=[
            jax.ShapeDtypeStruct(projected.shape, jnp.bfloat16),
            jax.ShapeDtypeStruct((8, width), jnp.float32),
        ],
        compiler_params=pltpu.CompilerParams(vmem_limit_bytes=24 << 20),
        name="attend_back",
    )(projected, projected, projected, attn, grad_attn, mask, cosine, sine, *gains)


def pack_kernel(*refs):
    out = refs[-1]
    start = 0
    for matrix in refs[:-1]:
        n = matrix.shape[1] // out.shape[0]
        for d in range(out.shape[0]):
            out[d, :, start : start + n] = matrix[:, d * n : (d + 1) * n]
        start += n


def pack(matrices, count):
    rows = matrices[0].shape[0]
    cols = sum(m.shape[1] for m in matrices) // count
    return pl.pallas_call(
        pack_kernel,
        grid=(1,),
        in_specs=[pl.BlockSpec(m.shape, lambda i: (0, 0)) for m in matrices],
        out_specs=pl.BlockSpec((count, rows, cols), lambda i: (0, 0, 0)),
        out_shape=jax.ShapeDtypeStruct((count, rows, cols), matrices[0].dtype),
        name="pack",
    )(*matrices)


def unpack_kernel(sizes, pieces_ref, *outs):
    start = 0
    for out, n in zip(outs, sizes):
        for d in range(pieces_ref.shape[0]):
            piece = pieces_ref[d, :, start : start + n]
            out[:, d * n : (d + 1) * n] = piece.astype(jnp.float32)
        start += n


def unpack(pieces, sizes):
    count, rows, _ = pieces.shape
    return pl.pallas_call(
        functools.partial(unpack_kernel, tuple(sizes)),
        out_shape=[jax.ShapeDtypeStruct((rows, count * n), jnp.float32) for n in sizes],
        compiler_params=pltpu.CompilerParams(vmem_limit_bytes=8 << 20),
        name="unpack",
    )(pieces)


def can_slice(mesh):
    seq_size = mesh.shape["seq"]
    ctx_size = mesh.shape["ctx"]
    return seq_size == 8 and ctx_size == 4


def swap_ctx(array, bit, seq_size, ctx_size):
    pairs = [
        (s * ctx_size + c, s * ctx_size + (c ^ bit))
        for s in range(seq_size)
        for c in range(ctx_size)
    ]
    return lax.ppermute(array, ("seq", "ctx"), pairs)


def sliced_layer(*arrays):
    return sliced_body(*arrays)


def sliced_body(
    hidden_in,
    positions,
    norm1_gain,
    w_query,
    key_weight_matrix,
    value_weight_matrix,
    query_gain,
    key_gain,
    w_out,
    norm2_gain,
    w_gate,
    w_up,
    w_down,
    cotangent,
):
    seq_size = lax.axis_size("seq")
    ctx_size = lax.axis_size("ctx")
    my_seq = lax.axis_index("seq")
    my_ctx = lax.axis_index("ctx")
    row_count = hidden_in.shape[1]
    width = hidden_in.shape[2]
    head_width = query_gain.shape[0]
    heads = w_query.shape[1] // head_width // ctx_size
    kv_heads = key_weight_matrix.shape[1] // head_width // ctx_size
    hidden_cols = w_gate.shape[1] // ctx_size
    bits = [1 << b for b in reversed(range(ctx_size.bit_length() - 1))]
    block = width // seq_size
    half = seq_size // 2

    def spot_of(s):
        return jnp.where(s % 2 == 0, s // 2, seq_size - 1 - s // 2)

    ring = list(range(0, seq_size, 2)) + list(range(seq_size - 1, 0, -2))
    spot = spot_of(my_seq)
    offsets = [0]
    for k in range(1, half):
        offsets += [-k, k]
    offsets.append(half)
    place = {o % seq_size: k for k, o in enumerate(offsets)}
    order = []
    for o in offsets:
        r = (spot + (o + seq_size)) % seq_size
        order.append(jnp.where(r < half, 2 * r, 2 * (seq_size - 1 - r) + 1))
    unorder = []
    for s in range(seq_size):
        r = (ring.index(s) + seq_size - spot) % seq_size
        near = jnp.where(r < half, 2 * r, 2 * (seq_size - r) - 1)
        unorder.append(jnp.where(r == half, seq_size - 1, near))

    def pick_blocks(array, which):
        return jnp.concatenate(
            [
                lax.dynamic_slice_in_dim(array, which[k] * block, block, array.ndim - 1)
                for k in range(seq_size)
            ],
            array.ndim - 1,
        )

    def shift(array, by):
        pairs = [
            (
                ring[r] * ctx_size + c,
                ring[(r + by) % seq_size] * ctx_size + c,
            )
            for r in range(seq_size)
            for c in range(ctx_size)
        ]
        return lax.ppermute(array, ("seq", "ctx"), pairs)

    def swap(array, bit):
        return swap_ctx(array, bit, seq_size, ctx_size)

    def exchange(pieces):
        rest = pieces.shape[1:]
        state = pieces.reshape((2,) * len(bits) + rest)
        for axis, bit in enumerate(bits):
            mine = (my_ctx & bit) != 0
            low = lax.index_in_dim(state, 0, axis, False)
            high = lax.index_in_dim(state, 1, axis, False)
            keep = jnp.where(mine, high, low)
            got = swap(jnp.where(mine, low, high), bit)
            source = lax.broadcasted_iota(jnp.int32, state.shape, axis) == mine.astype(jnp.int32)
            state = jnp.where(source, jnp.expand_dims(keep, axis), jnp.expand_dims(got, axis))
        return state.reshape((ctx_size,) + rest)

    def join_tokens(array):
        for bit in bits:
            array = jnp.concatenate((array, swap(array, bit)), 0)
        return array

    def sum_tokens(array):
        for bit in reversed(bits):
            rows = array.shape[0] // 2
            got = swap(array[rows:].astype(jnp.bfloat16), bit)
            array = array[:rows] + got.astype(jnp.float32)
        return array

    def after(array, *others):
        return lax.optimization_barrier((array, *others))[0] if others else array

    def gather_rows(own, gates):
        blocks = [own]
        ahead = back = own
        for k in range(1, half):
            ahead = shift(ahead, 1)
            back = shift(back, -1)
            ahead, back = lax.optimization_barrier((ahead, back) + tuple(gates.get(k, ())))[:2]
            blocks += [ahead, back]
        middle = block // 2
        ahead = shift(ahead[:middle], 1)
        back = shift(back[middle:], -1)
        blocks.append(jnp.concatenate((ahead, back), 0))
        return blocks

    def scatter_rows(pairs):
        def rows_of(offset, sent):
            k = place[offset % seq_size]
            return jnp.concatenate(
                [dot(x[:, k * block : (k + 1) * block], after(g, *sent), first) for x, g in pairs],
                1,
            )

        middle = block // 2
        far = rows_of(half, ()).astype(jnp.bfloat16)
        sends = [(far[:middle], far[middle:])]
        for k in range(half - 1, -1, -1):
            ahead = shift(sends[-1][0], 1).astype(jnp.float32)
            back = shift(sends[-1][1], -1).astype(jnp.float32)
            if k == 0:
                total = rows_of(0, sends[-1]) + ahead + back
                return total.astype(jnp.bfloat16), sends
            to_ahead = rows_of(k, sends[-1])
            to_back = rows_of(-k, sends[-1])
            if k == half - 1:
                to_ahead = jnp.concatenate((to_ahead[:middle] + ahead, to_ahead[middle:]), 0)
                to_back = jnp.concatenate((to_back[:middle], to_back[middle:] + back), 0)
            else:
                to_ahead = to_ahead + ahead
                to_back = to_back + back
            to_ahead = to_ahead.astype(jnp.bfloat16)
            to_back = to_back.astype(jnp.bfloat16)
            sends.append(lax.optimization_barrier((to_ahead, to_back)))

    def own_rows(matrices):
        pieces = pack(matrices, ctx_size)
        return exchange(pieces).reshape(block, -1)

    def sum_all(array):
        for bit in reversed(bits):
            array = array + swap(array, bit)
        bit = 1
        while bit < seq_size:
            pairs = [
                (s * ctx_size + c, (s ^ bit) * ctx_size + c)
                for s in range(seq_size)
                for c in range(ctx_size)
            ]
            array = array + lax.ppermute(array, ("seq", "ctx"), pairs)
            bit *= 2
        return array

    def collect(rows, sizes):
        pieces = exchange(rows.reshape(ctx_size, -1, rows.shape[1]))
        return unpack(pieces, sizes)

    def dot(left, right, dims):
        return lax.dot_general(left, right, (dims, ((), ())), preferred_element_type=jnp.float32)

    plain = ((1,), (0,))
    last = ((1,), (1,))
    first = ((0,), (0,))

    gain1 = pick_blocks(norm1_gain, order)
    gain2 = pick_blocks(norm2_gain, order)
    inputs = pick_blocks(hidden_in[0], order).astype(jnp.float32)
    cot_own = pick_blocks(cotangent[0], order)
    factor1, unit1 = unit_rows(inputs)
    digits = jnp.where(
        jnp.arange(head_width)[None, :] < head_width // 2,
        positions[0][:, None] // 128,
        positions[0][:, None] % 128,
    ).astype(jnp.bfloat16)
    attn_own = own_rows([w_query, key_weight_matrix, value_weight_matrix, w_out])
    mlp_own = own_rows([w_gate, w_up, w_down])
    joined = join_tokens(
        jnp.concatenate(
            ((unit1 * gain1).astype(jnp.bfloat16), cot_own, digits), 1
        ),
    )
    normed1 = joined[:, :width]
    cot = joined[:, width : 2 * width]
    digits = joined[:, 2 * width :].astype(jnp.float32)
    position_ids = (digits[:, 0] * 128.0 + digits[:, head_width // 2]).astype(jnp.int32)

    query_cols = heads * head_width
    kv_cols = kv_heads * head_width
    owners = [0]
    for bit in bits:
        owners = owners + [o ^ bit for o in owners]
    index = jnp.concatenate(
        [(my_ctx ^ o) * row_count + jnp.arange(row_count, dtype=jnp.int32) for o in owners]
    )
    begin = index - position_ids
    allowed = (index[:, None] <= index[None, :]) & (index[:, None] >= begin[None, :])
    mask = jnp.where(allowed, 0.0, -jnp.inf)
    cosine, sine = rope_tables(position_ids, head_width)
    cosine = jnp.concatenate((cosine, cosine), 1)
    sine = jnp.concatenate((-sine, sine), 1)

    attn_blocks = gather_rows(attn_own, {half - 1: (mask, cosine, sine)})
    mlp_blocks = gather_rows(mlp_own, {})
    attn_full = jnp.concatenate(attn_blocks, 0)
    mlp_full = jnp.concatenate(mlp_blocks, 0)
    joint = attn_full[:, : query_cols + 2 * kv_cols]
    out_cols = attn_full[:, query_cols + 2 * kv_cols :]
    gate_up = mlp_full[:, : 2 * hidden_cols]
    down = mlp_full[:, 2 * hidden_cols :]

    projected = dot(normed1, joint, plain)
    gains = (query_gain[None, :], key_gain[None, :])
    attn = attend(projected, mask, cosine, sine, gains, heads, kv_heads)

    residual = inputs + sum_tokens(dot(attn, out_cols, last))
    factor2, unit2 = unit_rows(residual)
    normed2 = join_tokens((unit2 * gain2).astype(jnp.bfloat16))
    gate_up_out = dot(normed2, gate_up, plain)
    gate = gate_up_out[:, :hidden_cols]
    upward = gate_up_out[:, hidden_cols:]
    sigmoid = jax.nn.sigmoid(gate)
    activation = gate * sigmoid
    hidden_units = (activation * upward).astype(jnp.bfloat16)
    grad_hid = dot(cot, down, plain)
    grad_gate = grad_hid * upward * sigmoid * (1.0 + gate * (1.0 - sigmoid))
    grad_up = grad_hid * activation
    grad_gate_up = jnp.concatenate((grad_gate, grad_up), 1).astype(jnp.bfloat16)
    back_mlp = dot(grad_gate_up, gate_up, last)
    grad_normed2 = sum_tokens(back_mlp)
    gain2_local = jnp.sum(grad_normed2 * unit2, 0)
    grad_residual = cot_own.astype(jnp.float32) + unit_back(grad_normed2 * gain2, factor2, unit2)
    grad_residual_b = join_tokens(grad_residual.astype(jnp.bfloat16))
    grad_attn = dot(grad_residual_b, out_cols, plain).astype(jnp.bfloat16)
    mlp_rows, _ = scatter_rows([(cot, hidden_units), (normed2, grad_gate_up)])
    grad_joint, gain_local = attend_back(
        projected, attn, grad_attn, mask, cosine, sine, gains, heads, kv_heads
    )
    grad_down_w, grad_gate_w, grad_up_w = collect(mlp_rows, [hidden_cols] * 3)
    attn_rows, sends = scatter_rows([(grad_residual_b, attn), (normed1, grad_joint)])
    grad_out_w, grad_query_w, grad_key_w, grad_value_w = collect(
        attn_rows, [query_cols, query_cols, kv_cols, kv_cols]
    )
    late_units = after(hidden_units, *sends[2])
    late_out = dot(late_units, down, last)
    out_hidden = (residual + sum_tokens(late_out)).astype(jnp.bfloat16)

    back_joint = dot(grad_joint, joint, last)
    grad_normed1 = sum_tokens(back_joint)
    gain1_local = jnp.sum(grad_normed1 * unit1, 0)
    grad_inputs = (grad_residual + unit_back(grad_normed1 * gain1, factor1, unit1)).astype(
        jnp.bfloat16
    )
    gain_sizes = [width, width, head_width, head_width]
    gain_rows = sum_all(
        jnp.concatenate(
            (
                pick_blocks(gain1_local, unorder),
                pick_blocks(gain2_local, unorder),
                gain_local[0],
                gain_local[1],
            )
        ).reshape(-1, head_width),
    ).reshape(-1)
    gain_totals = []
    start = 0
    for n in gain_sizes:
        gain_totals.append(gain_rows[start : start + n])
        start += n
    return (
        pick_blocks(out_hidden, unorder)[None],
        pick_blocks(grad_inputs, unorder)[None],
        grad_query_w,
        grad_key_w,
        grad_value_w,
        grad_out_w,
        grad_gate_w,
        grad_up_w,
        grad_down_w,
        gain_totals[0],
        gain_totals[1],
        gain_totals[2],
        gain_totals[3],
    )


def solution(mesh):
    placed = (
        P("seq", "ctx", None),
        P("seq", "ctx"),
        P(),
        P(("seq", "ctx"), None),
        P(("seq", "ctx"), None),
        P(("seq", "ctx"), None),
        P(),
        P(),
        P(("seq", "ctx"), None),
        P(),
        P(("seq", "ctx"), None),
        P(("seq", "ctx"), None),
        P(("seq", "ctx"), None),
        P("seq", "ctx", None),
    )
    layer = sliced_layer if can_slice(mesh) else gathered_layer
    return jax.shard_map(
        layer,
        mesh=mesh,
        in_specs=placed,
        out_specs=(
            P("seq", "ctx", None),
            P("seq", "ctx", None),
            P(("seq", "ctx"), None),
            P(("seq", "ctx"), None),
            P(("seq", "ctx"), None),
            P(("seq", "ctx"), None),
            P(("seq", "ctx"), None),
            P(("seq", "ctx"), None),
            P(("seq", "ctx"), None),
            P(),
            P(),
            P(),
            P(),
        ),
        check_vma=False,
    )
```
